32 devices in a mesh: section: 4 (over x, core), dp: 8 (over z, y).
Axes of the slice: x: 2, y: 2, z: 4, core: 2. Of those that a mesh axis runs over, the one named last changes fastest.
Arguments:
- examples: bfloat16 [2, 1024, 2048], P(None, 'dp'), may hold values from -6 to 6
- arriving: float32 [4, 1024, 2048], P('section', 'dp'), may hold values from -6 to 6
- returning: float32 [4, 1024, 2048], P('section', 'dp'), may hold values from -6 to 6
- stash: bfloat16 [4, 2, 1024, 2048], P('section', None, 'dp'), may hold values from -6 to 6
- plan: int32 [4, 2], P('section'), may hold values from 0 to 1, each once within a row
- forward_expert_routes: int32 [4, 2, 1024, 8], P('section', None, 'dp'), may hold values from 0 to 127, as said below
- backward_expert_routes: int32 [4, 2, 1024, 8], P('section', None, 'dp'), may hold values from 0 to 127, as said below
- input_norm_gain: float32 [4, 2048], P('section'), may hold values from 0.1 to 1.9
- router: bfloat16 [4, 2048, 128], P('section'), may hold values from -0.125 to 0.125
- frozen_gate_weight: bfloat16 [4, 2048, 384], P('section'), may hold values from -0.125 to 0.125
- frozen_up_weight: bfloat16 [4, 2048, 384], P('section'), may hold values from -0.125 to 0.125
- frozen_down_weight: bfloat16 [4, 384, 2048], P('section'), may hold values from -0.3125 to 0.3125
- down_factors: bfloat16 [4, 2048, 64], P('section'), may hold values from -0.125 to 0.125
- up_factors: bfloat16 [4, 2, 32, 384], P('section'), may hold values from -0.5 to 0.5
Outputs:
- next_acts: float32 [4, 1024, 2048], P('section', 'dp')
- next_grads: float32 [4, 1024, 2048], P('section', 'dp')
- grad_a: float32 [4, 2048, 64], P('section', 'dp')
- grad_b: float32 [4, 2, 32, 384], P('section', None, None, 'dp')
The draws below stay inside these ranges and needn't reach their ends.
Inputs may be any that keep to these rules, and one draw needn't show every extreme that they name: forward_expert_routes[..., 0] is 0 for every token: each section holds expert 0 of its layer. The other 7 entries of a token are distinct numbers from 1 to 127. `backward_expert_routes`: as forward_expert_routes: entry 0 is 0, the rest distinct from 1 to 127. `plan`: each section's row is a permutation of 0 to 1.
All inputs are finite; a program needn't handle non-finite values.
Results may differ from the reference program's by a relative error of at most 0.015.
Values sent between devices are 32-bit elements; how exact they have to be, the bound alone decides.
A program may use at most 64 MiB of HBM per device.

```python
import jax
import jax.numpy as jnp
from jax import lax

MODEL_WIDTH = 2048
HIDDEN_UNITS = 384
EXPERTS = 128
TOPK = 8
ADAPTER_RANK = 32
TICKS = 2
TOK = 128
RELAY_SECTIONS = 4
TOKENS = 1024
N_DP = 8


def routes_common(key):
    row_count = RELAY_SECTIONS * TICKS * TOKENS
    keys = jax.random.split(key, row_count)

    def pick_row(row_key):
        return jax.random.permutation(row_key, EXPERTS - 1)[:TOPK - 1] + 1
    others = jax.vmap(pick_row)(keys).astype(jnp.int32)
    leading = jnp.zeros((row_count, 1), jnp.int32)
    return jnp.concatenate([leading, others], axis=1).reshape(RELAY_SECTIONS, TICKS, TOKENS, TOPK)


def draw_forward_expert_routes(key, part):
    return routes_common(jax.random.fold_in(key, 11))


def draw_backward_expert_routes(key, part):
    return routes_common(jax.random.fold_in(key, 23))


def block_scale(stream_key, shape, cuts, low, high):
    gain = 1.0
    for dim, parts in cuts:
        heights = jax.random.uniform(jax.random.fold_in(jax.random.fold_in(stream_key, 6), dim), (parts,), jnp.float32, low / len(cuts), high / len(cuts))
        gain = gain * jnp.repeat(jnp.exp(heights), shape[dim] // parts).reshape((-1,) + (1,) * (len(shape) - 1 - dim))
    return gain


def gaussian(key, extent, scale, limit, pieces=(), held_as=jnp.bfloat16):
    gain = block_scale(key, extent, pieces, -0.22, 0.18) if pieces else 1.0
    drawn = jax.random.normal(key, extent, jnp.float32) * scale * gain
    return jnp.minimum(jnp.maximum(drawn, -limit), limit).astype(held_as)


def setup_inputs(seed: int = 0) -> dict:
    splits = jax.random.split(jax.random.key(seed), 15)
    return {
        "examples": gaussian(splits[0], (TICKS, TOKENS, MODEL_WIDTH), 1.0, 6.0, ((1, 8),)),
        "arriving": gaussian(splits[1], (RELAY_SECTIONS, TOKENS, MODEL_WIDTH), 1.0, 6.0, ((0, 4), (1, 8)), jnp.float32),
        "returning": gaussian(splits[2], (RELAY_SECTIONS, TOKENS, MODEL_WIDTH), 1.0, 6.0, ((0, 4), (1, 8)), jnp.float32),
        "stash": gaussian(splits[3], (RELAY_SECTIONS, TICKS, TOKENS, MODEL_WIDTH), 1.0, 6.0, ((0, 4), (2, 8))),
        "plan": jax.vmap(lambda own: jax.random.permutation(own, TICKS))(jax.random.split(splits[4], RELAY_SECTIONS)).reshape((RELAY_SECTIONS, TICKS)).astype(jnp.int32),
        "forward_expert_routes": draw_forward_expert_routes(jax.random.fold_in(splits[14], 71), 0),
        "backward_expert_routes": draw_backward_expert_routes(jax.random.fold_in(splits[14], 71), 0),
        "input_norm_gain": jnp.clip(1.0 + 0.18 * jax.random.normal(splits[7], (RELAY_SECTIONS, MODEL_WIDTH), jnp.float32), 0.1, 1.9),
        "router": gaussian(splits[8], (RELAY_SECTIONS, MODEL_WIDTH, EXPERTS), MODEL_WIDTH ** -0.5, 0.125, ((0, 4),)),
        "frozen_gate_weight": gaussian(splits[9], (RELAY_SECTIONS, MODEL_WIDTH, HIDDEN_UNITS), MODEL_WIDTH ** -0.5, 0.125, ((0, 4),)),
        "frozen_up_weight": gaussian(splits[10], (RELAY_SECTIONS, MODEL_WIDTH, HIDDEN_UNITS), MODEL_WIDTH ** -0.5, 0.125, ((0, 4),)),
        "frozen_down_weight": gaussian(splits[11], (RELAY_SECTIONS, HIDDEN_UNITS, MODEL_WIDTH), HIDDEN_UNITS ** -0.5, 0.3125, ((0, 4),)),
        "down_factors": gaussian(splits[12], (RELAY_SECTIONS, MODEL_WIDTH, 2 * ADAPTER_RANK), MODEL_WIDTH ** -0.5, 0.125, ((0, 4),)),
        "up_factors": gaussian(splits[13], (RELAY_SECTIONS, 2, ADAPTER_RANK, HIDDEN_UNITS), (4 * ADAPTER_RANK) ** -0.5, 0.5, ((0, 4),)),
    }


adapter_scale = 2.0

def apply_layer(inputs, routes, frozen, adapter_down, adapter_up):
    gain_vec, router_w, gate_matrix, up_matrix, down_w = frozen
    inputs_f = inputs.astype(jnp.float32)
    mean_square = lax.optimization_barrier(jnp.mean(inputs_f * inputs_f, axis=-1, keepdims=True))
    normalized_input = (inputs_f * lax.rsqrt(mean_square + 1e-06) * gain_vec).astype(jnp.bfloat16)
    logits = jnp.dot(normalized_input, router_w, preferred_element_type=jnp.float32)
    one_hot = (routes[:, :, None] == jnp.arange(router_w.shape[1], dtype=jnp.int32)[None, None, :]).astype(jnp.float32)
    picked = jnp.einsum('tke,te->tk', one_hot, logits.astype(jnp.float32))
    scores = jnp.exp(picked)
    weight = scores[:, 0] / lax.optimization_barrier(jnp.sum(scores, axis=-1))
    factor_rank = adapter_down.shape[1] // 2
    reduced_rank_output = jnp.dot(normalized_input, adapter_down.astype(jnp.bfloat16), preferred_element_type=jnp.float32).astype(jnp.bfloat16)
    up_factor_matrix = adapter_up.astype(jnp.bfloat16)
    gate_preactivation = jnp.dot(normalized_input, gate_matrix, preferred_element_type=jnp.float32) + adapter_scale * jnp.dot(reduced_rank_output[:, :factor_rank], up_factor_matrix[0], preferred_element_type=jnp.float32)
    up_preactivation = jnp.dot(normalized_input, up_matrix, preferred_element_type=jnp.float32) + adapter_scale * jnp.dot(reduced_rank_output[:, factor_rank:], up_factor_matrix[1], preferred_element_type=jnp.float32)
    hidden = (jax.nn.silu(gate_preactivation) * up_preactivation).astype(jnp.bfloat16)
    branch = jnp.dot(hidden, down_w, preferred_element_type=jnp.float32)
    return inputs_f + weight[:, None] * branch

def normalizer(grad_a, grad_b):
    entries = grad_a.size + grad_b.size
    mean_square = (jnp.sum(grad_a * grad_a) + jnp.sum(grad_b * grad_b)) / entries
    return lax.rsqrt(mean_square + 1e-06)

def example_step(inputs, routes, cotangent, frozen, adapter_down, adapter_up):

    def closed(values, first_a, first_b):
        return apply_layer(values, routes, frozen, first_a, first_b)
    result, pullback = jax.vjp(closed, inputs, adapter_down, adapter_up)
    d_input, grad_a, grad_b = pullback(cotangent)
    factor = normalizer(grad_a, grad_b)
    return (d_input, factor * grad_a, factor * grad_b)

def reference(examples, arriving, returning, stash, plan, forward_expert_routes, backward_expert_routes, input_norm_gain, router, frozen_gate_weight, frozen_up_weight, frozen_down_weight, down_factors, up_factors):
    ex_blocks = examples.reshape(TICKS, N_DP, TOK, MODEL_WIDTH).astype(jnp.float32)
    fwd_in = arriving.reshape(RELAY_SECTIONS, N_DP, TOK, MODEL_WIDTH)
    back_in = returning.reshape(RELAY_SECTIONS, N_DP, TOK, MODEL_WIDTH)
    stash_blocks = stash.reshape(RELAY_SECTIONS, TICKS, N_DP, TOK, MODEL_WIDTH)
    fwd_routes = forward_expert_routes.reshape(RELAY_SECTIONS, TICKS, N_DP, TOK, TOPK)
    bwd_routes = backward_expert_routes.reshape(RELAY_SECTIONS, TICKS, N_DP, TOK, TOPK)
    frozen = (input_norm_gain, router, frozen_gate_weight, frozen_up_weight, frozen_down_weight)
    adapter_down = down_factors.astype(jnp.float32)
    adapter_up = up_factors.astype(jnp.float32)
    section_ids = jnp.arange(RELAY_SECTIONS, dtype=jnp.int32)
    first_mask = (section_ids == 0)[:, None, None, None]
    last_mask = (section_ids == RELAY_SECTIONS - 1)[:, None, None, None]
    forward_all = jax.vmap(jax.vmap(apply_layer, in_axes=(0, 0, None, None, None)))
    backward_all = jax.vmap(jax.vmap(example_step, in_axes=(0, 0, 0, None, None, None)))
    total_a = jnp.zeros(adapter_down.shape, jnp.float32)
    total_b = jnp.zeros(adapter_up.shape, jnp.float32)
    for tick_index in range(TICKS):
        source = jnp.where(first_mask, ex_blocks[tick_index][None], fwd_in)
        routes_now = fwd_routes[:, tick_index]
        output = forward_all(source, routes_now, frozen, adapter_down, adapter_up)
        slot_index = plan[:, tick_index].astype(jnp.int32)
        stashed = stash_blocks[section_ids, slot_index].astype(jnp.float32)
        stashed_routes = bwd_routes[section_ids, slot_index]
        primal_in = jnp.where(last_mask, source, stashed)
        primal_routes = jnp.where(last_mask, routes_now, stashed_routes)
        loss_grad = output - ex_blocks[tick_index][None]
        incoming = jnp.where(last_mask, loss_grad, back_in)
        d_input, share_a, share_b = backward_all(primal_in, primal_routes, incoming, frozen, adapter_down, adapter_up)
        total_a = total_a + lax.optimization_barrier(jnp.sum(share_a, axis=1))
        total_b = total_b + lax.optimization_barrier(jnp.sum(share_b, axis=1))
        fwd_in = jnp.concatenate([jnp.zeros_like(output[:1]), output[:-1]], axis=0)
        back_in = jnp.concatenate([d_input[1:], jnp.zeros_like(d_input[:1])], axis=0)
    divisor = TICKS * N_DP
    return (fwd_in.reshape(RELAY_SECTIONS, TOKENS, MODEL_WIDTH), back_in.reshape(RELAY_SECTIONS, TOKENS, MODEL_WIDTH), total_a / divisor, total_b / divisor)
```

```python
import functools

import jax
import jax.numpy as jnp
from jax import lax
from jax.experimental import pallas as pl
from jax.experimental.pallas import tpu as pltpu
from jax.sharding import PartitionSpec as P

MESH = pl.DeviceIdType.MESH
F32 = jnp.float32
BF16 = jnp.bfloat16
ROWS = 16
TILE = 256
PIECES = 4
LANES = 128


def dot(a, b):
    return jnp.dot(a, b, preferred_element_type=F32)


def dot_nt(a, b):
    return lax.dot_general(a, b, (((1,), (1,)), ((), ())), preferred_element_type=F32)


def dot_tn(a, b):
    return lax.dot_general(a, b, (((0,), (0,)), ((), ())), preferred_element_type=F32)


def kernel(
    sections, replicas,
    plan_hbm, ex_hbm, arr_hbm, ret_hbm, stash_hbm, froutes_hbm, broutes_hbm, gain_hbm,
    router_hbm, gate_hbm, up_hbm, down_hbm, a_hbm, b_hbm,
    acts_out, grads_out, ga_out, gb_out,
    plan_ref, ex, arr, ret, stash, froutes, broutes, gain, b_ref, w1, wd, a_t, bd,
    x_buf, n_buf, rs_buf, pre, h_buf, low_buf, logit_buf, prob_buf, ls_buf, d_buf, corr,
    y_tx, dx_tx, fin, bin_, tot, pair_rx, peer_rx, zero,
    load_sem, y_send, y_recv, dx_send, dx_recv, pair_send, pair_recv, peer_send, peer_recv,
    zero_sem,
):
    s = lax.axis_index("section")
    me = lax.axis_index("dp")
    is_first = s == 0
    is_last = s == sections - 1
    not_first = s > 0
    not_last = s < sections - 1
    ticks, tok, width = ex.shape
    hidden = wd.shape[0]
    experts = router_hbm.shape[2]
    rank2 = a_t.shape[0]
    two_h = 2 * hidden
    main = two_h + experts
    full = main + rank2
    back_first = jnp.logical_and(jnp.logical_and(lax.rem(s, 2) == 0, not_last), not_first)
    fore_first = jnp.logical_not(back_first)

    half = replicas // 2
    side = lax.rem(me, 2)
    place = lax.div(me, 2)
    partner = me + 1 - 2 * side

    barrier = pltpu.get_barrier_semaphore()
    for d in (1, sections - 1):
        pl.semaphore_signal(
            barrier, inc=1, device_id={"section": lax.rem(s + d, sections)}, device_id_type=MESH
        )
    pl.semaphore_signal(barrier, inc=1, device_id={"dp": partner}, device_id_type=MESH)
    for d in range(1, half):
        pl.semaphore_signal(
            barrier, inc=1, device_id={"dp": lax.rem(me + 2 * d, replicas)}, device_id_type=MESH
        )

    pairs = {
        "plan": (plan_hbm, plan_ref),
        "gain": (gain_hbm, gain),
        "arr": (arr_hbm.at[0], arr),
        "ex": (ex_hbm, ex),
        "stash": (stash_hbm.at[0], stash),
        "gate": (gate_hbm.at[0], w1.at[:, 0:hidden]),
        "up": (up_hbm.at[0], w1.at[:, hidden:two_h]),
        "router": (router_hbm.at[0], w1.at[:, two_h:main]),
        "a": (a_hbm.at[0], a_t),
        "b": (b_hbm.at[0], b_ref),
        "fr": (froutes_hbm.at[0], froutes),
        "br": (broutes_hbm.at[0], broutes),
        "down": (down_hbm.at[0], wd),
        "ret": (ret_hbm.at[0], ret),
    }
    loads = {
        name: pltpu.make_async_copy(a, b, load_sem.at[i])
        for i, (name, (a, b)) in enumerate(pairs.items())
    }

    def start(*names):
        for name in names:
            loads[name].start()

    def wait(*names):
        for name in names:
            loads[name].wait()

    def normalize(at, take):
        def body(i, carry):
            rows = pl.ds(pl.multiple_of(i * ROWS, ROWS), ROWS)
            x = take(rows)
            x_buf[at, rows, :] = x
            r = lax.rsqrt(jnp.mean(x * x, axis=-1, keepdims=True) + 1e-6)
            n_buf[at, rows, :] = (x * r * gain[...]).astype(BF16)
            rs_buf[at, rows, :] = jnp.broadcast_to(r, (ROWS, rs_buf.shape[2]))
            return carry

        lax.fori_loop(0, tok // ROWS, body, 0, unroll=True)

    def project(at, first=False):
        n = n_buf[at]
        if first:
            wait("gate", "up")
        for j in range(two_h // TILE):
            cols = slice(j * TILE, (j + 1) * TILE)
            pre[at, :, cols] = dot(n, w1[:, cols])
        if first:
            wait("router")
        tail = dot(n, w1[:, two_h:full])
        logit_buf[at] = tail[:, 0:experts]
        low_buf[at] = tail[:, experts:experts + rank2].astype(BF16)

    def hidden_of(at, routes):
        logits = logit_buf[at]
        low = low_buf[at]
        expert = lax.broadcasted_iota(jnp.int32, (experts, tok), 0)
        chosen = expert == routes[0:1, :]
        for k in range(1, routes.shape[0]):
            chosen = jnp.logical_or(chosen, expert == routes[k:k + 1, :])
        chosen = jnp.where(chosen, 1.0, 0.0).T > 0.5
        scores = jnp.where(chosen, jnp.exp(logits), 0.0)
        prob = scores / jnp.sum(scores, axis=-1, keepdims=True)
        prob_buf[at] = prob
        mean = jnp.sum(prob * logits, axis=-1, keepdims=True)
        ls_buf[at] = jnp.broadcast_to(logits[:, 0:1] - mean, ls_buf.shape[1:])
        pre[at] = pre[at] + 2.0 * dot(low, bd[...])
        g = pre[at, :, 0:hidden]
        h_buf[at] = (g * jax.nn.sigmoid(g) * pre[at, :, hidden:two_h]).astype(BF16)

    piece = width // PIECES

    def send_y(t, p):
        cols = slice(p * piece, (p + 1) * piece)
        dst = fin.at[t, :, cols] if t < ticks - 1 else acts_out.at[0, :, cols]
        return pltpu.make_async_remote_copy(
            y_tx.at[t, :, cols], dst, y_send.at[t, p], y_recv.at[t, p],
            device_id={"section": lax.min(s + 1, sections - 1)}, device_id_type=MESH,
        )

    def send_dx(t, p):
        cols = slice(p * piece, (p + 1) * piece)
        dst = bin_.at[t, :, cols] if t < ticks - 1 else grads_out.at[0, :, cols]
        return pltpu.make_async_remote_copy(
            dx_tx.at[t, :, cols], dst, dx_send.at[t, p], dx_recv.at[t, p],
            device_id={"section": lax.max(s - 1, 0)}, device_id_type=MESH,
        )

    def turn(k):
        return lax.rem(place + k + 1, half)

    def to_partner(k):
        return pltpu.make_async_remote_copy(
            tot.at[(1 - side) * half + turn(k)], pair_rx.at[k], pair_send.at[k], pair_recv.at[k],
            device_id={"dp": partner}, device_id_type=MESH,
        )

    def to_peer(k):
        return pltpu.make_async_remote_copy(
            tot.at[side * half + turn(k)], peer_rx.at[k], peer_send.at[k], peer_recv.at[k],
            device_id={"dp": 2 * turn(k) + side}, device_id_type=MESH,
        )

    wa, wb = ga_out.shape[1], gb_out.shape[3]
    half_b = wb // 2
    a_rows = rank2 * (wa // LANES)

    def source(t, rows):
        arrived = arr[rows, :] if t == 0 else fin[t - 1, rows, :]
        return jnp.where(is_first, ex[t, rows, :].astype(F32), arrived)

    def prepare_forward(t):
        if t > 0:
            @pl.when(not_first)
            def _():
                for p in range(PIECES):
                    send_y(t - 1, p).wait_recv()

        normalize(0, lambda rows: source(t, rows))

    def finish_forward(t):
        hidden_of(0, froutes[t])
        own = prob_buf[0, :, 0:1]
        for p in range(PIECES):
            cols = slice(p * piece, (p + 1) * piece)
            y_tx[t, :, cols] = x_buf[0, :, cols] + own * dot(h_buf[0], wd[:, cols])

            @pl.when(not_last)
            def _():
                send_y(t, p).start()

    def forward(t):
        prepare_forward(t)
        project(0)
        finish_forward(t)

    def prepare_recompute(t):
        slot = plan_ref[0, t]
        normalize(1 + t, lambda rows: stash[slot, rows, :].astype(F32))

    def finish_recompute(t):
        hidden_of(1 + t, broutes[plan_ref[0, t]])

    def backward(t):
        kept = jnp.where(is_last, 0, 1 + t)

        def cotangent(cols):
            incoming = ret[:, cols] if t == 0 else bin_[t - 1, :, cols]
            return jnp.where(is_last, y_tx[t, :, cols] - ex[t, :, cols].astype(F32), incoming)

        q = None
        for p in range(PIECES):
            if t > 0:
                @pl.when(not_last)
                def _():
                    send_dx(t - 1, p).wait_recv()

            cols = slice(p * piece, (p + 1) * piece)
            part = dot_nt(cotangent(cols).astype(BF16), wd[:, cols])
            q = part if q is None else q + part
        prob = prob_buf[kept]
        own = prob[:, 0:1]
        d_own = jnp.sum(q * h_buf[kept].astype(F32), axis=-1, keepdims=True)
        d_hidden = own * q
        g = pre[kept, :, 0:hidden]
        u = pre[kept, :, hidden:two_h]
        sg = jax.nn.sigmoid(g)
        d_u = d_hidden * (g * sg)
        d_g = d_hidden * u * (sg * (1.0 + g * (1.0 - sg)))
        d_buf[:, 0:hidden] = d_g.astype(BF16)
        d_buf[:, hidden:two_h] = d_u.astype(BF16)
        lane = lax.broadcasted_iota(jnp.int32, (tok, experts), 1)
        d_pick = d_own * own
        d_buf[:, two_h:main] = (d_pick * (jnp.where(lane == 0, 1.0, 0.0) - prob)).astype(BF16)
        inner = jnp.sum(d_g * g + d_u * u, axis=-1, keepdims=True) + d_pick * ls_buf[kept, :, 0:1]
        r = rs_buf[kept, :, 0:1]
        corr[...] = jnp.broadcast_to(inner * r * r * (1.0 / width), corr.shape)
        d_low = (2.0 * dot_nt(d_buf[:, 0:two_h], bd[...])).astype(BF16)
        d_buf[:, main:full] = d_low

        def gradients():
            grad_b = 2.0 * dot_tn(low_buf[kept], d_buf[:, 0:two_h])
            row = lax.broadcasted_iota(jnp.int32, (rank2, hidden), 0)
            grad_b = jnp.where(row < rank2 // 2, grad_b[:, 0:hidden], grad_b[:, hidden:two_h])
            grad_a = dot_tn(d_buf[:, main:full], n_buf[kept])
            entries = rank2 * width + rank2 * hidden
            square = jnp.sum(grad_a * grad_a) + jnp.sum(grad_b * grad_b)
            factor = lax.rsqrt(jnp.full((1, 1), square, F32) / entries + 1e-6) * (
                1.0 / (ticks * replicas)
            )
            grad_b = grad_b * factor
            both = jnp.concatenate([grad_b, pltpu.roll(grad_b, hidden - half_b, 1)], axis=0).T
            for n in range(replicas):
                block = (n % 2) * half + n // 2
                parts = [
                    (i * rank2, rank2, grad_a[:, c:c + LANES] * factor)
                    for i, c in enumerate(range(n * wa, (n + 1) * wa, LANES))
                ]
                parts.append((a_rows, half_b, both[n * wb:n * wb + half_b, :]))
                for at, count, value in parts:
                    if t == 0:
                        tot[block, at:at + count, :] = value
                    else:
                        tot[block, at:at + count, :] = tot[block, at:at + count, :] + value

        def spread():
            @pl.when(not_first)
            def _():
                rs = rs_buf[kept, :, 0:1]
                cr = corr[:, 0:1]
                for p in range(PIECES):
                    for c in range(p * piece, (p + 1) * piece, TILE):
                        cols = slice(c, c + TILE)
                        m = dot_nt(d_buf[...], w1[cols, :]) * gain[:, cols]
                        dx_tx[t, :, cols] = (
                            cotangent(cols) + rs * m - cr * x_buf[kept, :, cols]
                        )
                    send_dx(t, p).start()

        if t < ticks - 1:
            spread()
            gradients()
        else:
            gradients()
            for k in range(half):
                to_partner(k).start()
            spread()

    def exchange():
        for k in range(half):
            to_partner(k).wait_recv()
            block = side * half + turn(k)
            tot[block] = tot[block] + pair_rx[k]
            if k < half - 1:
                to_peer(k).start()

    start("gain", "a", "b")

    @pl.when(back_first)
    def _():
        start("plan", "stash", "br")

    @pl.when(fore_first)
    def _():
        @pl.when(is_first)
        def _():
            start("ex")

        @pl.when(not_first)
        def _():
            start("arr")

        start("fr")

    start("gate", "up", "router", "down")

    @pl.when(back_first)
    def _():
        start("ret")

    bd[...] = jnp.zeros_like(bd)
    wait("gain", "a", "b")
    bd[0:rank2 // 2, 0:hidden] = b_ref[0]
    bd[rank2 // 2:rank2, hidden:two_h] = b_ref[1]
    w1[:, main:full] = a_t[...].astype(F32).T.astype(BF16)

    @pl.when(back_first)
    def _():
        wait("plan", "stash", "br")
        prepare_recompute(0)

    @pl.when(fore_first)
    def _():
        @pl.when(is_first)
        def _():
            wait("ex")

        @pl.when(not_first)
        def _():
            wait("arr")

        wait("fr")
        prepare_forward(0)

    project(jnp.where(back_first, 1, 0), first=True)
    wait("down")

    @pl.when(back_first)
    def _():
        start("arr", "fr")
        finish_recompute(0)
        wait("ret")

    @pl.when(fore_first)
    def _():
        @pl.when(not_last)
        def _():
            start("plan", "stash", "br", "ret")

        @pl.when(jnp.logical_and(is_last, not_first))
        def _():
            start("ex")

    pl.semaphore_wait(barrier, half + 2)

    @pl.when(fore_first)
    def _():
        finish_forward(0)

        @pl.when(not_last)
        def _():
            wait("plan", "stash", "br", "ret")
            prepare_recompute(0)
            project(1)
            finish_recompute(0)

        @pl.when(jnp.logical_and(is_last, not_first))
        def _():
            wait("ex")

    backward(0)

    @pl.when(back_first)
    def _():
        wait("arr", "fr")
        forward(0)

    edge_acts = pltpu.make_async_copy(zero, acts_out.at[0], zero_sem.at[0])
    edge_grads = pltpu.make_async_copy(zero, grads_out.at[0], zero_sem.at[0])
    at_edge = jnp.logical_or(is_first, is_last)

    @pl.when(at_edge)
    def _():
        zero[...] = jnp.zeros_like(zero)

    @pl.when(is_first)
    def _():
        edge_acts.start()

    @pl.when(jnp.logical_and(is_last, not_first))
    def _():
        edge_grads.start()

    for t in range(1, ticks):
        @pl.when(fore_first)
        def _():
            forward(t)

        @pl.when(not_last)
        def _():
            prepare_recompute(t)
            project(1 + t)
            finish_recompute(t)

        backward(t)
        if t == ticks - 1:
            exchange()

        @pl.when(back_first)
        def _():
            forward(t)

    total = tot[side * half + place]
    for k in range(half - 1):
        to_peer(k).wait_recv()
        total = total + peer_rx[k]
    for i in range(wa // LANES):
        ga_out[:, i * LANES:(i + 1) * LANES] = total[i * rank2:(i + 1) * rank2, :]
    pad = jnp.zeros((LANES - half_b, LANES), F32)
    turned = jnp.concatenate([total[a_rows:a_rows + half_b, :], pad], axis=0).T
    lane = lax.broadcasted_iota(jnp.int32, (rank2, LANES), 1)
    sum_b = jnp.where(
        lane < half_b, turned[0:rank2, :], pltpu.roll(turned[rank2:2 * rank2, :], half_b, 1)
    )
    gb_out[0, 0] = sum_b[0:rank2 // 2, 0:wb]
    gb_out[0, 1] = sum_b[rank2 // 2:rank2, 0:wb]

    for k in range(half):
        to_partner(k).wait_send()
        if k < half - 1:
            to_peer(k).wait_send()

    @pl.when(not_first)
    def _():
        for p in range(PIECES):
            send_y(ticks - 1, p).wait_recv()
            for t in range(ticks):
                send_dx(t, p).wait_send()

    @pl.when(not_last)
    def _():
        for p in range(PIECES):
            send_dx(ticks - 1, p).wait_recv()
            for t in range(ticks):
                send_y(t, p).wait_send()

    @pl.when(is_first)
    def _():
        edge_acts.wait()

    @pl.when(jnp.logical_and(is_last, not_first))
    def _():
        edge_grads.wait()


def deliver(*refs):
    count = len(refs) // 2
    sem = refs[-1]
    copies = [
        pltpu.make_async_copy(refs[i], refs[count + i], sem.at[i]) for i in range(count)
    ]
    for copy in copies:
        copy.start()
    for copy in copies:
        copy.wait()


def shards(sections, replicas, *args):
    (examples, arriving, returning, stash, plan, forward_routes, backward_routes, gain,
     router, gate_w, up_w, down_w, down_factors, up_factors) = args
    ticks, tok, width = examples.shape
    hidden = gate_w.shape[2]
    experts = router.shape[2]
    rank2 = down_factors.shape[2]
    topk = forward_routes.shape[3]
    hbm = pl.BlockSpec(memory_space=pltpu.HBM)
    any_ = pl.BlockSpec(memory_space=pl.ANY)
    vmem = pl.BlockSpec(memory_space=pltpu.VMEM)
    wa, wb = width // replicas, hidden // replicas
    half = replicas // 2
    share = rank2 * (wa // LANES) + (wb // 2 + 7) // 8 * 8
    dma = pltpu.SemaphoreType.DMA
    vm = pltpu.VMEM
    outs = (
        jax.ShapeDtypeStruct((1, tok, width), F32),
        jax.ShapeDtypeStruct((1, tok, width), F32),
        jax.ShapeDtypeStruct((rank2, wa), F32),
        jax.ShapeDtypeStruct((1, 2, rank2 // 2, wb), F32),
    )
    operands = [
        pltpu.with_memory_space_constraint(value, pltpu.HBM)
        for value in (
            plan, examples, arriving, returning, stash, jnp.swapaxes(forward_routes, 2, 3),
            jnp.swapaxes(backward_routes, 2, 3), gain, router, gate_w, up_w, down_w,
            jnp.swapaxes(down_factors, 1, 2), up_factors,
        )
    ]
    results = pl.pallas_call(
        functools.partial(kernel, sections, replicas),
        out_shape=outs,
        in_specs=[hbm] * 14,
        out_specs=(any_, any_, vmem, vmem),
        scratch_shapes=[
            pltpu.SMEM((1, ticks), jnp.int32),
            vm((ticks, tok, width), BF16),
            vm((tok, width), F32),
            vm((tok, width), F32),
            vm((ticks, tok, width), BF16),
            vm((ticks, topk, tok), jnp.int32),
            vm((ticks, topk, tok), jnp.int32),
            vm((1, width), F32),
            vm((2, rank2 // 2, hidden), BF16),
            vm((width, 2 * hidden + experts + rank2), BF16),
            vm((hidden, width), BF16),
            vm((rank2, width), BF16),
            vm((rank2, 2 * hidden), BF16),
            vm((1 + ticks, tok, width), F32),
            vm((1 + ticks, tok, width), BF16),
            vm((1 + ticks, tok, LANES), F32),
            vm((1 + ticks, tok, 2 * hidden), F32),
            vm((1 + ticks, tok, hidden), BF16),
            vm((1 + ticks, tok, rank2), BF16),
            vm((1 + ticks, tok, experts), F32),
            vm((1 + ticks, tok, experts), F32),
            vm((1 + ticks, tok, LANES), F32),
            vm((tok, 2 * hidden + experts + rank2), BF16),
            vm((tok, LANES), F32),
            vm((ticks, tok, width), F32),
            vm((ticks, tok, width), F32),
            vm((ticks - 1, tok, width), F32),
            vm((ticks - 1, tok, width), F32),
            vm((replicas, share, LANES), F32),
            vm((half, share, LANES), F32),
            vm((half - 1, share, LANES), F32),
            vm((tok, width), F32),
            dma((14,)),
            dma((ticks, PIECES)),
            dma((ticks, PIECES)),
            dma((ticks, PIECES)),
            dma((ticks, PIECES)),
            dma((half,)),
            dma((half,)),
            dma((half - 1,)),
            dma((half - 1,)),
            dma((1,)),
        ],
        compiler_params=pltpu.CompilerParams(
            collective_id=0, has_side_effects=True, vmem_limit_bytes=44 * 1024 * 1024
        ),
    )(*operands)
    acts, grads, ga, gb = pl.pallas_call(
        deliver,
        out_shape=outs,
        in_specs=[any_] * 4,
        out_specs=(any_,) * 4,
        scratch_shapes=[dma((4,))],
        compiler_params=pltpu.CompilerParams(vmem_limit_bytes=1024 * 1024),
    )(*results)
    return acts, grads, ga.T[None], gb


def solution(mesh):
    in_specs = (
        P(None, "dp", None),
        P("section", "dp", None),
        P("section", "dp", None),
        P("section", None, "dp", None),
        P("section", None),
        P("section", None, "dp", None),
        P("section", None, "dp", None),
        P("section", None),
        P("section", None, None),
        P("section", None, None),
        P("section", None, None),
        P("section", None, None),
        P("section", None, None),
        P("section", None, None, None),
    )
    out_specs = (
        P("section", "dp", None),
        P("section", "dp", None),
        P("section", "dp", None),
        P("section", None, None, "dp"),
    )
    body = functools.partial(shards, mesh.shape["section"], mesh.shape["dp"])
    return jax.shard_map(body, mesh=mesh, in_specs=in_specs, out_specs=out_specs, check_vma=False)
```

```python
import functools

import jax
import jax.numpy as jnp
from jax import lax
from jax.experimental import pallas as pl
from jax.experimental.pallas import tpu as pltpu
from jax.sharding import PartitionSpec as P

MESH = pl.DeviceIdType.MESH
F32 = jnp.float32
BF16 = jnp.bfloat16
ROWS = 16
TILE = 256
PIECES = 4
LANES = 128


def dot(a, b):
    return jnp.dot(a, b, preferred_element_type=F32)


def dot_nt(a, b):
    return lax.dot_general(a, b, (((1,), (1,)), ((), ())), preferred_element_type=F32)


def dot_tn(a, b):
    return lax.dot_general(a, b, (((0,), (0,)), ((), ())), preferred_element_type=F32)


def kernel(
    sections, replicas,
    plan_hbm, ex_hbm, arr_hbm, ret_hbm, stash_hbm, froutes_hbm, broutes_hbm, gain_hbm,
    router_hbm, gate_hbm, up_hbm, down_hbm, a_hbm, b_hbm,
    acts_out, grads_out, ga_out, gb_out,
    plan_ref, ex, arr, ret, stash, froutes, broutes, gain, b_ref, w1, wd, a_t, bd,
    x_buf, n_buf, rs_buf, pre, h_buf, low_buf, prob_buf, ls_buf, gc_buf, d_buf, corr,
    y_tx, dx_tx, fin, bin_, tot, pair_rx, peer_rx, zero,
    load_sem, y_send, y_recv, dx_send, dx_recv, pair_send, pair_recv, peer_send, peer_recv,
    zero_sem,
):
    s = lax.axis_index("section")
    me = lax.axis_index("dp")
    is_first = s == 0
    is_last = s == sections - 1
    not_first = s > 0
    not_last = s < sections - 1
    ticks, tok, width = ex.shape
    hidden = wd.shape[0]
    experts = router_hbm.shape[2]
    rank2 = a_t.shape[0]
    two_h = 2 * hidden
    main = two_h + experts
    full = main + rank2
    back_first = jnp.logical_and(jnp.logical_and(lax.rem(s, 2) == 0, not_last), not_first)
    fore_first = jnp.logical_not(back_first)

    half = replicas // 2
    side = lax.rem(me, 2)
    place = lax.div(me, 2)
    partner = me + 1 - 2 * side

    barrier = pltpu.get_barrier_semaphore()
    for d in (1, sections - 1):
        pl.semaphore_signal(
            barrier, inc=1, device_id={"section": lax.rem(s + d, sections)}, device_id_type=MESH
        )
    pl.semaphore_signal(barrier, inc=1, device_id={"dp": partner}, device_id_type=MESH)
    for d in range(1, half):
        pl.semaphore_signal(
            barrier, inc=1, device_id={"dp": lax.rem(me + 2 * d, replicas)}, device_id_type=MESH
        )

    pairs = {
        "plan": (plan_hbm, plan_ref),
        "gain": (gain_hbm, gain),
        "arr": (arr_hbm.at[0], arr),
        "ex": (ex_hbm, ex),
        "stash": (stash_hbm.at[0], stash),
        "gate": (gate_hbm.at[0], w1.at[:, 0:hidden]),
        "up": (up_hbm.at[0], w1.at[:, hidden:two_h]),
        "router": (router_hbm.at[0], w1.at[:, two_h:main]),
        "a": (a_hbm.at[0], a_t),
        "b": (b_hbm.at[0], b_ref),
        "fr": (froutes_hbm.at[0], froutes),
        "br": (broutes_hbm.at[0], broutes),
        "down": (down_hbm.at[0], wd),
        "ret": (ret_hbm.at[0], ret),
    }
    loads = {
        name: pltpu.make_async_copy(a, b, load_sem.at[i])
        for i, (name, (a, b)) in enumerate(pairs.items())
    }

    def start(*names):
        for name in names:
            loads[name].start()

    def wait(*names):
        for name in names:
            loads[name].wait()

    def normalize(at, take):
        def body(i, carry):
            rows = pl.ds(pl.multiple_of(i * ROWS, ROWS), ROWS)
            x = take(rows)
            x_buf[at, rows, :] = x
            r = lax.rsqrt(jnp.mean(x * x, axis=-1, keepdims=True) + 1e-6)
            n_buf[at, rows, :] = (x * r * gain[...]).astype(BF16)
            rs_buf[at, rows, :] = jnp.broadcast_to(r, (ROWS, rs_buf.shape[2]))
            return carry

        lax.fori_loop(0, tok // ROWS, body, 0, unroll=True)

    def mark(at, routes):
        expert = lax.broadcasted_iota(jnp.int32, (experts, tok), 0)
        chosen = expert == routes[0:1, :]
        for k in range(1, routes.shape[0]):
            chosen = jnp.logical_or(chosen, expert == routes[k:k + 1, :])
        prob_buf[at] = jnp.where(chosen, 1.0, 0.0).T

    def project(at, first=False):
        n = n_buf[at]
        if first:
            wait("router")
        tail = dot(n, w1[:, two_h:full])
        logits = tail[:, 0:experts]
        low = tail[:, experts:experts + rank2].astype(BF16)
        low_buf[at] = low
        scores = jnp.where(prob_buf[at] > 0.5, jnp.exp(logits), 0.0)
        prob = scores / jnp.sum(scores, axis=-1, keepdims=True)
        prob_buf[at] = prob
        mean = jnp.sum(prob * logits, axis=-1, keepdims=True)
        ls_buf[at] = jnp.broadcast_to(logits[:, 0:1] - mean, ls_buf.shape[1:])
        if first:
            wait("gate")
        for j in range(two_h // TILE):
            cols = slice(j * TILE, (j + 1) * TILE)
            if first and (j + 1) * TILE > hidden and j * TILE <= hidden:
                wait("up")
            pre[at, :, cols] = dot(n, w1[:, cols]) + 2.0 * dot(low, bd[:, cols])
        g = pre[at, :, 0:hidden]
        u = pre[at, :, hidden:two_h]
        sg = jax.nn.sigmoid(g)
        silu = g * sg
        h_buf[at] = (silu * u).astype(BF16)
        slope = u * (sg * (1.0 + g * (1.0 - sg)))
        pre[at, :, 0:hidden] = slope
        pre[at, :, hidden:two_h] = silu
        gc_buf[at] = slope * g + silu * u

    piece = width // PIECES

    def send_y(t, p):
        cols = slice(p * piece, (p + 1) * piece)
        dst = fin.at[t, :, cols] if t < ticks - 1 else acts_out.at[0, :, cols]
        return pltpu.make_async_remote_copy(
            y_tx.at[t, :, cols], dst, y_send.at[t, p], y_recv.at[t, p],
            device_id={"section": lax.min(s + 1, sections - 1)}, device_id_type=MESH,
        )

    cuts = [0, TILE] + [p * piece for p in range(1, PIECES + 1)]
    parts_dx = len(cuts) - 1

    def send_dx(t, p):
        cols = slice(cuts[p], cuts[p + 1])
        dst = bin_.at[t, :, cols] if t < ticks - 1 else grads_out.at[0, :, cols]
        return pltpu.make_async_remote_copy(
            dx_tx.at[t, :, cols], dst, dx_send.at[t, p], dx_recv.at[t, p],
            device_id={"section": lax.max(s - 1, 0)}, device_id_type=MESH,
        )

    def turn(k):
        return lax.rem(place + k + 1, half)

    def to_partner(k):
        return pltpu.make_async_remote_copy(
            tot.at[(1 - side) * half + turn(k)], pair_rx.at[k], pair_send.at[k], pair_recv.at[k],
            device_id={"dp": partner}, device_id_type=MESH,
        )

    def to_peer(k):
        return pltpu.make_async_remote_copy(
            tot.at[side * half + turn(k)], peer_rx.at[k], peer_send.at[k], peer_recv.at[k],
            device_id={"dp": 2 * turn(k) + side}, device_id_type=MESH,
        )

    wa, wb = ga_out.shape[1], gb_out.shape[3]
    half_b = wb // 2
    a_rows = rank2 * (wa // LANES)

    def source(t, rows):
        arrived = arr[rows, :] if t == 0 else fin[t - 1, rows, :]
        return jnp.where(is_first, ex[t, rows, :].astype(F32), arrived)

    def prepare_forward(t):
        if t > 0:
            @pl.when(not_first)
            def _():
                for p in range(PIECES):
                    send_y(t - 1, p).wait_recv()

        mark(0, froutes[t])
        normalize(0, lambda rows: source(t, rows))

    def finish_forward(t):
        own = prob_buf[0, :, 0:1]
        for p in range(PIECES):
            cols = slice(p * piece, (p + 1) * piece)
            y_tx[t, :, cols] = x_buf[0, :, cols] + own * dot(h_buf[0], wd[:, cols])

            @pl.when(not_last)
            def _():
                send_y(t, p).start()

    def forward(t):
        prepare_forward(t)
        project(0)
        finish_forward(t)

    def prepare_recompute(t):
        slot = plan_ref[0, t]
        mark(1 + t, broutes[slot])
        normalize(1 + t, lambda rows: stash[slot, rows, :].astype(F32))

    def backward(t):
        kept = jnp.where(is_last, 0, 1 + t)

        def cotangent(cols):
            incoming = ret[:, cols] if t == 0 else bin_[t - 1, :, cols]
            return jnp.where(is_last, y_tx[t, :, cols] - ex[t, :, cols].astype(F32), incoming)

        q = None
        for p in range(parts_dx):
            if t > 0:
                @pl.when(not_last)
                def _():
                    send_dx(t - 1, p).wait_recv()

            cols = slice(cuts[p], cuts[p + 1])
            part = dot_nt(cotangent(cols).astype(BF16), wd[:, cols])
            q = part if q is None else q + part
        prob = prob_buf[kept]
        own = prob[:, 0:1]
        d_own = jnp.sum(q * h_buf[kept].astype(F32), axis=-1, keepdims=True)
        d_hidden = own * q
        d_buf[:, 0:hidden] = (d_hidden * pre[kept, :, 0:hidden]).astype(BF16)
        d_buf[:, hidden:two_h] = (d_hidden * pre[kept, :, hidden:two_h]).astype(BF16)
        lane = lax.broadcasted_iota(jnp.int32, (tok, experts), 1)
        d_pick = d_own * own
        d_buf[:, two_h:main] = (d_pick * (jnp.where(lane == 0, 1.0, 0.0) - prob)).astype(BF16)
        inner = own * jnp.sum(q * gc_buf[kept], axis=-1, keepdims=True) + d_pick * ls_buf[kept, :, 0:1]
        r = rs_buf[kept, :, 0:1]
        corr[...] = jnp.broadcast_to(inner * r * r * (1.0 / width), corr.shape)
        d_low = (2.0 * dot_nt(d_buf[:, 0:two_h], bd[...])).astype(BF16)
        d_buf[:, main:full] = d_low

        def gradients():
            grad_b = 2.0 * dot_tn(low_buf[kept], d_buf[:, 0:two_h])
            row = lax.broadcasted_iota(jnp.int32, (rank2, hidden), 0)
            grad_b = jnp.where(row < rank2 // 2, grad_b[:, 0:hidden], grad_b[:, hidden:two_h])
            grad_a = dot_tn(d_buf[:, main:full], n_buf[kept])
            entries = rank2 * width + rank2 * hidden
            square = jnp.sum(grad_a * grad_a) + jnp.sum(grad_b * grad_b)
            factor = lax.rsqrt(jnp.full((1, 1), square, F32) / entries + 1e-6) * (
                1.0 / (ticks * replicas)
            )
            grad_b = grad_b * factor
            both = jnp.concatenate([grad_b, pltpu.roll(grad_b, hidden - half_b, 1)], axis=0).T
            for n in range(replicas):
                block = (n % 2) * half + n // 2
                parts = [
                    (i * rank2, rank2, grad_a[:, c:c + LANES] * factor)
                    for i, c in enumerate(range(n * wa, (n + 1) * wa, LANES))
                ]
                parts.append((a_rows, half_b, both[n * wb:n * wb + half_b, :]))
                for at, count, value in parts:
                    if t == 0:
                        tot[block, at:at + count, :] = value
                    else:
                        tot[block, at:at + count, :] = tot[block, at:at + count, :] + value

        def spread():
            @pl.when(not_first)
            def _():
                rs = rs_buf[kept, :, 0:1]
                cr = corr[:, 0:1]
                for p in range(parts_dx):
                    for c in range(cuts[p], cuts[p + 1], TILE):
                        cols = slice(c, c + TILE)
                        m = dot_nt(d_buf[...], w1[cols, :]) * gain[:, cols]
                        dx_tx[t, :, cols] = (
                            cotangent(cols) + rs * m - cr * x_buf[kept, :, cols]
                        )
                    send_dx(t, p).start()

        if t < ticks - 1:
            spread()
            gradients()
        else:
            gradients()
            for k in range(half):
                to_partner(k).start()
            spread()

    def exchange():
        for k in range(half):
            to_partner(k).wait_recv()
            block = side * half + turn(k)
            tot[block] = tot[block] + pair_rx[k]
            if k < half - 1:
                to_peer(k).start()

    start("gain", "a", "b")

    @pl.when(back_first)
    def _():
        start("plan", "br", "stash")

    @pl.when(fore_first)
    def _():
        start("fr")

        @pl.when(is_first)
        def _():
            start("ex")

        @pl.when(not_first)
        def _():
            start("arr")

    start("router", "gate", "up", "down")

    @pl.when(back_first)
    def _():
        start("ret")

    bd[...] = jnp.zeros_like(bd)
    wait("gain", "a", "b")
    bd[0:rank2 // 2, 0:hidden] = b_ref[0]
    bd[rank2 // 2:rank2, hidden:two_h] = b_ref[1]
    w1[:, main:full] = a_t[...].astype(F32).T.astype(BF16)

    @pl.when(back_first)
    def _():
        wait("plan", "stash", "br")
        prepare_recompute(0)

    @pl.when(fore_first)
    def _():
        @pl.when(is_first)
        def _():
            wait("ex")

        @pl.when(not_first)
        def _():
            wait("arr")

        wait("fr")
        prepare_forward(0)

    project(jnp.where(back_first, 1, 0), first=True)

    @pl.when(back_first)
    def _():
        start("arr", "fr")
        wait("ret")

    @pl.when(fore_first)
    def _():
        @pl.when(not_last)
        def _():
            start("plan", "stash", "br", "ret")

        @pl.when(jnp.logical_and(is_last, not_first))
        def _():
            start("ex")

    wait("down")
    pl.semaphore_wait(barrier, half + 2)

    @pl.when(fore_first)
    def _():
        finish_forward(0)

        @pl.when(not_last)
        def _():
            wait("plan", "stash", "br", "ret")
            prepare_recompute(0)
            project(1)

        @pl.when(jnp.logical_and(is_last, not_first))
        def _():
            wait("ex")

    backward(0)

    @pl.when(back_first)
    def _():
        wait("arr", "fr")
        forward(0)

    edge_acts = pltpu.make_async_copy(zero, acts_out.at[0], zero_sem.at[0])
    edge_grads = pltpu.make_async_copy(zero, grads_out.at[0], zero_sem.at[0])
    at_edge = jnp.logical_or(is_first, is_last)

    @pl.when(at_edge)
    def _():
        zero[...] = jnp.zeros_like(zero)

    @pl.when(is_first)
    def _():
        edge_acts.start()

    @pl.when(jnp.logical_and(is_last, not_first))
    def _():
        edge_grads.start()

    for t in range(1, ticks):
        @pl.when(fore_first)
        def _():
            forward(t)

        @pl.when(not_last)
        def _():
            prepare_recompute(t)
            project(1 + t)

        backward(t)
        if t == ticks - 1:
            exchange()

        @pl.when(back_first)
        def _():
            forward(t)

    total = tot[side * half + place]
    for k in range(half - 1):
        to_peer(k).wait_recv()
        total = total + peer_rx[k]
    for i in range(wa // LANES):
        ga_out[:, i * LANES:(i + 1) * LANES] = total[i * rank2:(i + 1) * rank2, :]
    pad = jnp.zeros((LANES - half_b, LANES), F32)
    turned = jnp.concatenate([total[a_rows:a_rows + half_b, :], pad], axis=0).T
    lane = lax.broadcasted_iota(jnp.int32, (rank2, LANES), 1)
    sum_b = jnp.where(
        lane < half_b, turned[0:rank2, :], pltpu.roll(turned[rank2:2 * rank2, :], half_b, 1)
    )
    gb_out[0, 0] = sum_b[0:rank2 // 2, 0:wb]
    gb_out[0, 1] = sum_b[rank2 // 2:rank2, 0:wb]

    for k in range(half):
        to_partner(k).wait_send()
        if k < half - 1:
            to_peer(k).wait_send()

    @pl.when(not_first)
    def _():
        for p in range(PIECES):
            send_y(ticks - 1, p).wait_recv()
        for p in range(parts_dx):
            for t in range(ticks):
                send_dx(t, p).wait_send()

    @pl.when(not_last)
    def _():
        for p in range(PIECES):
            for t in range(ticks):
                send_y(t, p).wait_send()
        for p in range(parts_dx):
            send_dx(ticks - 1, p).wait_recv()

    @pl.when(is_first)
    def _():
        edge_acts.wait()

    @pl.when(jnp.logical_and(is_last, not_first))
    def _():
        edge_grads.wait()


def deliver(*refs):
    count = len(refs) // 2
    sem = refs[-1]
    copies = [
        pltpu.make_async_copy(refs[i], refs[count + i], sem.at[i]) for i in range(count)
    ]
    for copy in copies:
        copy.start()
    for copy in copies:
        copy.wait()


def shards(sections, replicas, *args):
    (examples, arriving, returning, stash, plan, forward_routes, backward_routes, gain,
     router, gate_w, up_w, down_w, down_factors, up_factors) = args
    ticks, tok, width = examples.shape
    hidden = gate_w.shape[2]
    experts = router.shape[2]
    rank2 = down_factors.shape[2]
    topk = forward_routes.shape[3]
    hbm = pl.BlockSpec(memory_space=pltpu.HBM)
    any_ = pl.BlockSpec(memory_space=pl.ANY)
    vmem = pl.BlockSpec(memory_space=pltpu.VMEM)
    wa, wb = width // replicas, hidden // replicas
    half = replicas // 2
    share = rank2 * (wa // LANES) + (wb // 2 + 7) // 8 * 8
    dma = pltpu.SemaphoreType.DMA
    vm = pltpu.VMEM
    outs = (
        jax.ShapeDtypeStruct((1, tok, width), F32),
        jax.ShapeDtypeStruct((1, tok, width), F32),
        jax.ShapeDtypeStruct((rank2, wa), F32),
        jax.ShapeDtypeStruct((1, 2, rank2 // 2, wb), F32),
    )
    operands = [
        pltpu.with_memory_space_constraint(value, pltpu.HBM)
        for value in (
            plan, examples, arriving, returning, stash, jnp.swapaxes(forward_routes, 2, 3),
            jnp.swapaxes(backward_routes, 2, 3), gain, router, gate_w, up_w, down_w,
            jnp.swapaxes(down_factors, 1, 2), up_factors,
        )
    ]
    results = pl.pallas_call(
        functools.partial(kernel, sections, replicas),
        out_shape=outs,
        in_specs=[hbm] * 14,
        out_specs=(any_, any_, vmem, vmem),
        scratch_shapes=[
            pltpu.SMEM((1, ticks), jnp.int32),
            vm((ticks, tok, width), BF16),
            vm((tok, width), F32),
            vm((tok, width), F32),
            vm((ticks, tok, width), BF16),
            vm((ticks, topk, tok), jnp.int32),
            vm((ticks, topk, tok), jnp.int32),
            vm((1, width), F32),
            vm((2, rank2 // 2, hidden), BF16),
            vm((width, 2 * hidden + experts + rank2), BF16),
            vm((hidden, width), BF16),
            vm((rank2, width), BF16),
            vm((rank2, 2 * hidden), BF16),
            vm((1 + ticks, tok, width), F32),
            vm((1 + ticks, tok, width), BF16),
            vm((1 + ticks, tok, LANES), F32),
            vm((1 + ticks, tok, 2 * hidden), F32),
            vm((1 + ticks, tok, hidden), BF16),
            vm((1 + ticks, tok, rank2), BF16),
            vm((1 + ticks, tok, experts), F32),
            vm((1 + ticks, tok, LANES), F32),
            vm((1 + ticks, tok, hidden), F32),
            vm((tok, 2 * hidden + experts + rank2), BF16),
            vm((tok, LANES), F32),
            vm((ticks, tok, width), F32),
            vm((ticks, tok, width), F32),
            vm((ticks - 1, tok, width), F32),
            vm((ticks - 1, tok, width), F32),
            vm((replicas, share, LANES), F32),
            vm((half, share, LANES), F32),
            vm((half - 1, share, LANES), F32),
            vm((tok, width), F32),
            dma((14,)),
            dma((ticks, PIECES)),
            dma((ticks, PIECES)),
            dma((ticks, PIECES + 1)),
            dma((ticks, PIECES + 1)),
            dma((half,)),
            dma((half,)),
            dma((half - 1,)),
            dma((half - 1,)),
            dma((1,)),
        ],
        compiler_params=pltpu.CompilerParams(
            collective_id=0, has_side_effects=True, vmem_limit_bytes=44 * 1024 * 1024
        ),
    )(*operands)
    acts, grads, ga, gb = pl.pallas_call(
        deliver,
        out_shape=outs,
        in_specs=[any_] * 4,
        out_specs=(any_,) * 4,
        scratch_shapes=[dma((4,))],
        compiler_params=pltpu.CompilerParams(vmem_limit_bytes=1024 * 1024),
    )(*results)
    return acts, grads, ga.T[None], gb


def solution(mesh):
    in_specs = (
        P(None, "dp", None),
        P("section", "dp", None),
        P("section", "dp", None),
        P("section", None, "dp", None),
        P("section", None),
        P("section", None, "dp", None),
        P("section", None, "dp", None),
        P("section", None),
        P("section", None, None),
        P("section", None, None),
        P("section", None, None),
        P("section", None, None),
        P("section", None, None),
        P("section", None, None, None),
    )
    out_specs = (
        P("section", "dp", None),
        P("section", "dp", None),
        P("section", "dp", None),
        P("section", None, None, "dp"),
    )
    body = functools.partial(shards, mesh.shape["section"], mesh.shape["dp"])
    return jax.shard_map(body, mesh=mesh, in_specs=in_specs, out_specs=out_specs, check_vma=False)
```

```python
import functools

import jax
import jax.numpy as jnp
from jax import lax
from jax.experimental import pallas as pl
from jax.experimental.pallas import tpu as pltpu
from jax.sharding import PartitionSpec as P

MESH = pl.DeviceIdType.MESH
F32 = jnp.float32
BF16 = jnp.bfloat16
ROWS = 16
TILE = 256
PIECES = 4
LANES = 128


def dot(a, b):
    return jnp.dot(a, b, preferred_element_type=F32)


def dot_nt(a, b):
    return lax.dot_general(a, b, (((1,), (1,)), ((), ())), preferred_element_type=F32)


def dot_tn(a, b):
    return lax.dot_general(a, b, (((0,), (0,)), ((), ())), preferred_element_type=F32)


def kernel(
    sections, replicas,
    plan_hbm, ex_hbm, arr_hbm, ret_hbm, stash_hbm, froutes_hbm, broutes_hbm, gain_hbm,
    router_hbm, gate_hbm, up_hbm, down_hbm, a_hbm, b_hbm,
    acts_out, grads_out, ga_out, gb_out,
    plan_ref, ex, arr, ret, stash_low, stash_high, froutes, broutes, gain, b_ref, w1, wd, a_t, bd,
    x_buf, n_buf, rs_buf, pre, h_buf, low_buf, prob_buf, ls_buf, gc_buf, d_buf, corr,
    y_tx, dx_tx, fin, bin_, tot, pair_rx, peer_rx, zero,
    load_sem, y_send, y_recv, dx_send, dx_recv, pair_send, pair_recv, peer_send, peer_recv,
    zero_sem,
):
    s = lax.axis_index("section")
    me = lax.axis_index("dp")
    is_first = s == 0
    is_last = s == sections - 1
    not_first = s > 0
    not_last = s < sections - 1
    ticks, tok, width = ex.shape
    hidden = wd.shape[0]
    experts = router_hbm.shape[2]
    rank2 = a_t.shape[0]
    two_h = 2 * hidden
    main = two_h + experts
    full = main + rank2
    back_first = jnp.logical_and(jnp.logical_and(lax.rem(s, 2) == 0, not_last), not_first)
    fore_first = jnp.logical_not(back_first)

    half = replicas // 2
    side = lax.rem(me, 2)
    place = lax.div(me, 2)
    partner = me + 1 - 2 * side

    barrier = pltpu.get_barrier_semaphore()
    pairs = {
        "plan": (plan_hbm, plan_ref),
        "gain": (gain_hbm, gain),
        "arr": (arr_hbm.at[0], arr),
        "ex": (ex_hbm, ex),
        "stash0": (stash_hbm.at[0, :, 0:tok // 2], stash_low),
        "stash1": (stash_hbm.at[0, :, tok // 2:tok], stash_high),
        "gate": (gate_hbm.at[0], w1.at[:, 0:hidden]),
        "up": (up_hbm.at[0], w1.at[:, hidden:two_h]),
        "router": (router_hbm.at[0], w1.at[:, two_h:main]),
        "a": (a_hbm.at[0], a_t),
        "b": (b_hbm.at[0], b_ref),
        "fr": (froutes_hbm.at[0], froutes),
        "br": (broutes_hbm.at[0], broutes),
    }
    piece = width // PIECES
    for p in range(PIECES):
        cols = slice(p * piece, (p + 1) * piece)
        pairs["down%d" % p] = (down_hbm.at[0, :, cols], wd.at[:, cols])
        pairs["ret%d" % p] = (ret_hbm.at[0, :, cols], ret.at[:, cols])
    downs = ["down%d" % p for p in range(PIECES)]
    rets = ["ret%d" % p for p in range(PIECES)]
    loads = {
        name: pltpu.make_async_copy(a, b, load_sem.at[i])
        for i, (name, (a, b)) in enumerate(pairs.items())
    }

    def start(*names):
        for name in names:
            loads[name].start()

    def wait(*names):
        for name in names:
            loads[name].wait()

    def normalize(at, take, low=0, high=tok):
        def body(i, carry):
            rows = pl.ds(pl.multiple_of(low + i * ROWS, ROWS), ROWS)
            x = take(rows, pl.ds(pl.multiple_of(i * ROWS, ROWS), ROWS))
            x_buf[at, rows, :] = x
            r = lax.rsqrt(jnp.mean(x * x, axis=-1, keepdims=True) + 1e-6)
            n_buf[at, rows, :] = (x * r * gain[...]).astype(BF16)
            rs_buf[at, rows, :] = jnp.broadcast_to(r, (ROWS, rs_buf.shape[2]))
            return carry

        lax.fori_loop(0, (high - low) // ROWS, body, 0, unroll=True)

    def mark(at, routes):
        expert = lax.broadcasted_iota(jnp.int32, (experts, tok), 0)
        chosen = expert == routes[0:1, :]
        for k in range(1, routes.shape[0]):
            chosen = jnp.logical_or(chosen, expert == routes[k:k + 1, :])
        prob_buf[at] = jnp.where(chosen, 1.0, 0.0).T

    def project(at, first=False):
        n = n_buf[at]
        if first:
            wait("router", "gate")
        tail = dot(n, w1[:, two_h:full])
        logits = tail[:, 0:experts]
        low = tail[:, experts:experts + rank2].astype(BF16)
        low_buf[at] = low
        for j in range(two_h // TILE):
            cols = slice(j * TILE, (j + 1) * TILE)
            if j == 1:
                scores = jnp.where(prob_buf[at] > 0.5, jnp.exp(logits), 0.0)
                prob = scores / jnp.sum(scores, axis=-1, keepdims=True)
                prob_buf[at] = prob
                mean = jnp.sum(prob * logits, axis=-1, keepdims=True)
                ls_buf[at] = jnp.broadcast_to(logits[:, 0:1] - mean, ls_buf.shape[1:])
            if first and (j + 1) * TILE > hidden and j * TILE <= hidden:
                wait("up")
            pre[at, :, cols] = dot(n, w1[:, cols]) + 2.0 * dot(low, bd[:, cols])
        g = pre[at, :, 0:hidden]
        u = pre[at, :, hidden:two_h]
        sg = jax.nn.sigmoid(g)
        silu = g * sg
        h_buf[at] = (silu * u).astype(BF16)
        slope = u * (sg * (1.0 + g * (1.0 - sg)))
        pre[at, :, 0:hidden] = slope
        pre[at, :, hidden:two_h] = silu
        gc_buf[at] = slope * g + silu * u

    def send_y(t, p):
        cols = slice(p * piece, (p + 1) * piece)
        dst = fin.at[t, :, cols] if t < ticks - 1 else acts_out.at[0, :, cols]
        return pltpu.make_async_remote_copy(
            y_tx.at[t, :, cols], dst, y_send.at[t, p], y_recv.at[t, p],
            device_id={"section": lax.min(s + 1, sections - 1)}, device_id_type=MESH,
        )

    cuts = [0, LANES] + [p * piece for p in range(1, PIECES + 1)]
    parts_dx = len(cuts) - 1

    def send_dx(t, p):
        cols = slice(cuts[p], cuts[p + 1])
        dst = bin_.at[t, :, cols] if t < ticks - 1 else grads_out.at[0, :, cols]
        return pltpu.make_async_remote_copy(
            dx_tx.at[t, :, cols], dst, dx_send.at[t, p], dx_recv.at[t, p],
            device_id={"section": lax.max(s - 1, 0)}, device_id_type=MESH,
        )

    def turn(k):
        return lax.rem(place + k + 1, half)

    def to_partner(k):
        return pltpu.make_async_remote_copy(
            tot.at[(1 - side) * half + turn(k)], pair_rx.at[k], pair_send.at[k], pair_recv.at[k],
            device_id={"dp": partner}, device_id_type=MESH,
        )

    def to_peer(k):
        return pltpu.make_async_remote_copy(
            tot.at[side * half + turn(k)], peer_rx.at[k], peer_send.at[k], peer_recv.at[k],
            device_id={"dp": 2 * turn(k) + side}, device_id_type=MESH,
        )

    wa, wb = ga_out.shape[1], gb_out.shape[3]
    half_b = wb // 2
    a_rows = rank2 * (wa // LANES)

    def source(t, rows):
        arrived = arr[rows, :] if t == 0 else fin[t - 1, rows, :]
        return jnp.where(is_first, ex[t, rows, :].astype(F32), arrived)

    def prepare_forward(t):
        if t > 0:
            @pl.when(not_first)
            def _():
                for p in range(PIECES):
                    send_y(t - 1, p).wait_recv()

        mark(0, froutes[t])
        normalize(0, lambda rows, near: source(t, rows))

    def finish_forward(t):
        own = prob_buf[0, :, 0:1]
        for p in range(PIECES):
            cols = slice(p * piece, (p + 1) * piece)
            y_tx[t, :, cols] = x_buf[0, :, cols] + own * dot(h_buf[0], wd[:, cols])

            @pl.when(not_last)
            def _():
                send_y(t, p).start()

    def forward(t):
        prepare_forward(t)
        project(0)
        finish_forward(t)

    def prepare_recompute(t):
        slot = plan_ref[0, t]
        mark(1 + t, broutes[slot])
        for part, kept in enumerate((stash_low, stash_high)):
            if t == 0:
                wait("stash%d" % part)
            normalize(
                1 + t, lambda rows, near: kept[slot, near, :].astype(F32),
                part * (tok // 2), (part + 1) * (tok // 2),
            )

    def backward(t):
        kept = jnp.where(is_last, 0, 1 + t)

        def cotangent(cols):
            incoming = ret[:, cols] if t == 0 else bin_[t - 1, :, cols]
            return jnp.where(is_last, y_tx[t, :, cols] - ex[t, :, cols].astype(F32), incoming)

        q = None
        for p in range(PIECES):
            if t > 0:
                @pl.when(not_last)
                def _():
                    if p == 0:
                        send_dx(t - 1, 0).wait_recv()
                    send_dx(t - 1, p + 1).wait_recv()
            elif p == 0:
                @pl.when(back_first)
                def _():
                    wait(*downs, *rets)

            cols = slice(p * piece, (p + 1) * piece)
            part = dot_nt(cotangent(cols).astype(BF16), wd[:, cols])
            q = part if q is None else q + part
        prob = prob_buf[kept]
        own = prob[:, 0:1]
        d_own = jnp.sum(q * h_buf[kept].astype(F32), axis=-1, keepdims=True)
        d_hidden = own * q
        d_buf[:, 0:hidden] = (d_hidden * pre[kept, :, 0:hidden]).astype(BF16)
        d_buf[:, hidden:two_h] = (d_hidden * pre[kept, :, hidden:two_h]).astype(BF16)
        lane = lax.broadcasted_iota(jnp.int32, (tok, experts), 1)
        d_pick = d_own * own
        d_buf[:, two_h:main] = (d_pick * (jnp.where(lane == 0, 1.0, 0.0) - prob)).astype(BF16)
        inner = own * jnp.sum(q * gc_buf[kept], axis=-1, keepdims=True) + d_pick * ls_buf[kept, :, 0:1]
        r = rs_buf[kept, :, 0:1]
        corr[...] = jnp.broadcast_to(inner * r * r * (1.0 / width), corr.shape)
        d_low = (2.0 * dot_nt(d_buf[:, 0:two_h], bd[...])).astype(BF16)
        d_buf[:, main:full] = d_low

        def give(cols, m):
            dx_tx[t, :, cols] = (
                cotangent(cols) + rs_buf[kept, :, 0:1] * (m * gain[:, cols])
                - corr[:, 0:1] * x_buf[kept, :, cols]
            )

        head = slice(0, cuts[1])
        give(head, dot_nt(d_buf[:, 0:main], w1[head, 0:main]) + dot_nt(d_low, w1[head, main:full]))

        def gradients():
            grad_b = 2.0 * dot_tn(low_buf[kept], d_buf[:, 0:two_h])
            row = lax.broadcasted_iota(jnp.int32, (rank2, hidden), 0)
            grad_b = jnp.where(row < rank2 // 2, grad_b[:, 0:hidden], grad_b[:, hidden:two_h])
            grad_a = dot_tn(d_buf[:, main:full], n_buf[kept])
            entries = rank2 * width + rank2 * hidden
            square = jnp.sum(grad_a * grad_a) + jnp.sum(grad_b * grad_b)
            factor = lax.rsqrt(jnp.full((1, 1), square, F32) / entries + 1e-6) * (
                1.0 / (ticks * replicas)
            )
            grad_b = grad_b * factor
            both = jnp.concatenate([grad_b, pltpu.roll(grad_b, hidden - half_b, 1)], axis=0).T
            for n in range(replicas):
                block = (n % 2) * half + n // 2
                parts = [
                    (i * rank2, rank2, grad_a[:, c:c + LANES] * factor)
                    for i, c in enumerate(range(n * wa, (n + 1) * wa, LANES))
                ]
                parts.append((a_rows, half_b, both[n * wb:n * wb + half_b, :]))
                for at, count, value in parts:
                    if t == 0:
                        tot[block, at:at + count, :] = value
                    else:
                        tot[block, at:at + count, :] = tot[block, at:at + count, :] + value

        def spread():
            @pl.when(not_first)
            def _():
                for p in range(parts_dx):
                    for c in range(cuts[p], cuts[p + 1], TILE) if p > 0 else ():
                        cols = slice(c, min(c + TILE, cuts[p + 1]))
                        give(cols, dot_nt(d_buf[...], w1[cols, :]))
                    if t == 0 and p == 0:
                        @pl.when(back_first)
                        def _():
                            pl.semaphore_wait(barrier, half + 2)

                    send_dx(t, p).start()

        if t < ticks - 1:
            spread()
            gradients()
        else:
            gradients()
            for k in range(half):
                to_partner(k).start()
            spread()

    def exchange():
        for k in range(half):
            to_partner(k).wait_recv()
            block = side * half + turn(k)
            tot[block] = tot[block] + pair_rx[k]
            if k < half - 1:
                to_peer(k).start()

    start("gain", "a", "b")

    @pl.when(back_first)
    def _():
        start("plan", "br", "stash0", "stash1")

    @pl.when(fore_first)
    def _():
        start("fr")

        @pl.when(is_first)
        def _():
            start("ex")

        @pl.when(not_first)
        def _():
            start("arr")

    start("router", "gate", "up")

    @pl.when(back_first)
    def _():
        for p in range(PIECES):
            start("down%d" % p, "ret%d" % p)

    @pl.when(fore_first)
    def _():
        start(*downs)

    for d in (1, sections - 1):
        pl.semaphore_signal(
            barrier, inc=1, device_id={"section": lax.rem(s + d, sections)}, device_id_type=MESH
        )
    pl.semaphore_signal(barrier, inc=1, device_id={"dp": partner}, device_id_type=MESH)
    for d in range(1, half):
        pl.semaphore_signal(
            barrier, inc=1, device_id={"dp": lax.rem(me + 2 * d, replicas)}, device_id_type=MESH
        )

    bd[...] = jnp.zeros_like(bd)
    wait("gain", "a", "b")
    bd[0:rank2 // 2, 0:hidden] = b_ref[0]
    bd[rank2 // 2:rank2, hidden:two_h] = b_ref[1]
    w1[:, main:full] = a_t[...].astype(F32).T.astype(BF16)

    @pl.when(back_first)
    def _():
        wait("plan", "br")
        prepare_recompute(0)

    @pl.when(fore_first)
    def _():
        @pl.when(is_first)
        def _():
            wait("ex")

        @pl.when(not_first)
        def _():
            wait("arr")

        wait("fr")
        prepare_forward(0)

    project(jnp.where(back_first, 1, 0), first=True)

    @pl.when(back_first)
    def _():
        start("arr", "fr")

    @pl.when(fore_first)
    def _():
        @pl.when(not_last)
        def _():
            start("plan", "br", "stash0", "stash1", *rets)

        @pl.when(jnp.logical_and(is_last, not_first))
        def _():
            start("ex")

    @pl.when(fore_first)
    def _():
        wait(*downs)
        pl.semaphore_wait(barrier, half + 2)
        finish_forward(0)

        @pl.when(not_last)
        def _():
            wait("plan", "br", *rets)
            prepare_recompute(0)
            project(1)

        @pl.when(jnp.logical_and(is_last, not_first))
        def _():
            wait("ex")

    backward(0)

    @pl.when(back_first)
    def _():
        wait("arr", "fr")
        forward(0)

    edge_acts = pltpu.make_async_copy(zero, acts_out.at[0], zero_sem.at[0])
    edge_grads = pltpu.make_async_copy(zero, grads_out.at[0], zero_sem.at[0])
    at_edge = jnp.logical_or(is_first, is_last)

    @pl.when(at_edge)
    def _():
        zero[...] = jnp.zeros_like(zero)

    @pl.when(is_first)
    def _():
        edge_acts.start()

    @pl.when(jnp.logical_and(is_last, not_first))
    def _():
        edge_grads.start()

    for t in range(1, ticks):
        @pl.when(fore_first)
        def _():
            forward(t)

        @pl.when(not_last)
        def _():
            prepare_recompute(t)
            project(1 + t)

        backward(t)
        if t == ticks - 1:
            exchange()

        @pl.when(back_first)
        def _():
            forward(t)

    total = tot[side * half + place]
    for k in range(half - 1):
        to_peer(k).wait_recv()
        total = total + peer_rx[k]
    for i in range(wa // LANES):
        ga_out[:, i * LANES:(i + 1) * LANES] = total[i * rank2:(i + 1) * rank2, :]
    pad = jnp.zeros((LANES - half_b, LANES), F32)
    turned = jnp.concatenate([total[a_rows:a_rows + half_b, :], pad], axis=0).T
    lane = lax.broadcasted_iota(jnp.int32, (rank2, LANES), 1)
    sum_b = jnp.where(
        lane < half_b, turned[0:rank2, :], pltpu.roll(turned[rank2:2 * rank2, :], half_b, 1)
    )
    gb_out[0, 0] = sum_b[0:rank2 // 2, 0:wb]
    gb_out[0, 1] = sum_b[rank2 // 2:rank2, 0:wb]

    for k in range(half):
        to_partner(k).wait_send()
        if k < half - 1:
            to_peer(k).wait_send()

    @pl.when(not_first)
    def _():
        for p in range(PIECES):
            send_y(ticks - 1, p).wait_recv()
        for p in range(parts_dx):
            for t in range(ticks):
                send_dx(t, p).wait_send()

    @pl.when(not_last)
    def _():
        for p in range(PIECES):
            for t in range(ticks):
                send_y(t, p).wait_send()
        for p in range(parts_dx):
            send_dx(ticks - 1, p).wait_recv()

    @pl.when(is_first)
    def _():
        edge_acts.wait()

    @pl.when(jnp.logical_and(is_last, not_first))
    def _():
        edge_grads.wait()


def deliver(*refs):
    count = len(refs) // 2
    sem = refs[-1]
    copies = [
        pltpu.make_async_copy(refs[i], refs[count + i], sem.at[i]) for i in range(count)
    ]
    for copy in copies:
        copy.start()
    for copy in copies:
        copy.wait()


def shards(sections, replicas, *args):
    (examples, arriving, returning, stash, plan, forward_routes, backward_routes, gain,
     router, gate_w, up_w, down_w, down_factors, up_factors) = args
    ticks, tok, width = examples.shape
    hidden = gate_w.shape[2]
    experts = router.shape[2]
    rank2 = down_factors.shape[2]
    topk = forward_routes.shape[3]
    hbm = pl.BlockSpec(memory_space=pltpu.HBM)
    any_ = pl.BlockSpec(memory_space=pl.ANY)
    vmem = pl.BlockSpec(memory_space=pltpu.VMEM)
    wa, wb = width // replicas, hidden // replicas
    half = replicas // 2
    share = rank2 * (wa // LANES) + (wb // 2 + 7) // 8 * 8
    dma = pltpu.SemaphoreType.DMA
    vm = pltpu.VMEM
    outs = (
        jax.ShapeDtypeStruct((1, tok, width), F32),
        jax.ShapeDtypeStruct((1, tok, width), F32),
        jax.ShapeDtypeStruct((rank2, wa), F32),
        jax.ShapeDtypeStruct((1, 2, rank2 // 2, wb), F32),
    )
    operands = [
        pltpu.with_memory_space_constraint(value, pltpu.HBM)
        for value in (
            plan, examples, arriving, returning, stash, jnp.swapaxes(forward_routes, 2, 3),
            jnp.swapaxes(backward_routes, 2, 3), gain, router, gate_w, up_w, down_w,
            jnp.swapaxes(down_factors, 1, 2), up_factors,
        )
    ]
    results = pl.pallas_call(
        functools.partial(kernel, sections, replicas),
        out_shape=outs,
        in_specs=[hbm] * 14,
        out_specs=(any_, any_, vmem, vmem),
        scratch_shapes=[
            pltpu.SMEM((1, ticks), jnp.int32),
            vm((ticks, tok, width), BF16),
            vm((tok, width), F32),
            vm((tok, width), F32),
            vm((ticks, tok // 2, width), BF16),
            vm((ticks, tok // 2, width), BF16),
            vm((ticks, topk, tok), jnp.int32),
            vm((ticks, topk, tok), jnp.int32),
            vm((1, width), F32),
            vm((2, rank2 // 2, hidden), BF16),
            vm((width, 2 * hidden + experts + rank2), BF16),
            vm((hidden, width), BF16),
            vm((rank2, width), BF16),
            vm((rank2, 2 * hidden), BF16),
            vm((1 + ticks, tok, width), F32),
            vm((1 + ticks, tok, width), BF16),
            vm((1 + ticks, tok, LANES), F32),
            vm((1 + ticks, tok, 2 * hidden), F32),
            vm((1 + ticks, tok, hidden), BF16),
            vm((1 + ticks, tok, rank2), BF16),
            vm((1 + ticks, tok, experts), F32),
            vm((1 + ticks, tok, LANES), F32),
            vm((1 + ticks, tok, hidden), F32),
            vm((tok, 2 * hidden + experts + rank2), BF16),
            vm((tok, LANES), F32),
            vm((ticks, tok, width), F32),
            vm((ticks, tok, width), F32),
            vm((ticks - 1, tok, width), F32),
            vm((ticks - 1, tok, width), F32),
            vm((replicas, share, LANES), F32),
            vm((half, share, LANES), F32),
            vm((half - 1, share, LANES), F32),
            vm((tok, width), F32),
            dma((13 + 2 * PIECES,)),
            dma((ticks, PIECES)),
            dma((ticks, PIECES)),
            dma((ticks, PIECES + 1)),
            dma((ticks, PIECES + 1)),
            dma((half,)),
            dma((half,)),
            dma((half - 1,)),
            dma((half - 1,)),
            dma((1,)),
        ],
        compiler_params=pltpu.CompilerParams(
            collective_id=0, has_side_effects=True, vmem_limit_bytes=44 * 1024 * 1024
        ),
    )(*operands)
    acts, grads, ga, gb = pl.pallas_call(
        deliver,
        out_shape=outs,
        in_specs=[any_] * 4,
        out_specs=(any_,) * 4,
        scratch_shapes=[dma((4,))],
        compiler_params=pltpu.CompilerParams(vmem_limit_bytes=1024 * 1024),
    )(*results)
    return acts, grads, ga.T[None], gb


def solution(mesh):
    in_specs = (
        P(None, "dp", None),
        P("section", "dp", None),
        P("section", "dp", None),
        P("section", None, "dp", None),
        P("section", None),
        P("section", None, "dp", None),
        P("section", None, "dp", None),
        P("section", None),
        P("section", None, None),
        P("section", None, None),
        P("section", None, None),
        P("section", None, None),
        P("section", None, None),
        P("section", None, None, None),
    )
    out_specs = (
        P("section", "dp", None),
        P("section", "dp", None),
        P("section", "dp", None),
        P("section", None, None, "dp"),
    )
    body = functools.partial(shards, mesh.shape["section"], mesh.shape["dp"])
    return jax.shard_map(body, mesh=mesh, in_specs=in_specs, out_specs=out_specs, check_vma=False)
```

```python
import functools

import jax
import jax.numpy as jnp
from jax import lax
from jax.experimental import pallas as pl
from jax.experimental.pallas import tpu as pltpu
from jax.sharding import PartitionSpec as P

MESH = pl.DeviceIdType.MESH
F32 = jnp.float32
BF16 = jnp.bfloat16
ROWS = 16
TILE = 256
PIECES = 4
LANES = 128
EARLY = 1


def dot(a, b):
    return jnp.dot(a, b, preferred_element_type=F32)


def dot_nt(a, b):
    return lax.dot_general(a, b, (((1,), (1,)), ((), ())), preferred_element_type=F32)


def dot_tn(a, b):
    return lax.dot_general(a, b, (((0,), (0,)), ((), ())), preferred_element_type=F32)


def kernel(
    sections, replicas,
    plan_hbm, ex_hbm, arr_hbm, ret_hbm, stash_hbm, froutes_hbm, broutes_hbm, gain_hbm,
    router_hbm, gate_hbm, up_hbm, down_hbm, a_hbm, b_hbm,
    acts_out, grads_out, ga_out, gb_out,
    plan_ref, ex, arr, ret, stash_low, stash_high, froutes, broutes, gain, b_ref, w1, wd, a_t, bd,
    x_buf, n_buf, rs_buf, pre, h_buf, low_buf, prob_buf, ls_buf, gc_buf, q_buf, d_buf, corr,
    y_tx, dx_tx, fin, bin_, tot, pair_rx, peer_rx, zero,
    load_sem, y_send, y_recv, dx_send, dx_recv, pair_send, pair_recv, peer_send, peer_recv,
    zero_sem,
):
    s = lax.axis_index("section")
    me = lax.axis_index("dp")
    is_first = s == 0
    is_last = s == sections - 1
    not_first = s > 0
    not_last = s < sections - 1
    ticks, tok, width = ex.shape
    hidden = wd.shape[0]
    experts = router_hbm.shape[2]
    rank2 = a_t.shape[0]
    two_h = 2 * hidden
    main = two_h + experts
    full = main + rank2
    back_first = jnp.logical_and(jnp.logical_and(lax.rem(s, 2) == 0, not_last), not_first)
    fore_first = jnp.logical_not(back_first)

    half = replicas // 2
    side = lax.rem(me, 2)
    place = lax.div(me, 2)
    partner = me + 1 - 2 * side

    barrier = pltpu.get_barrier_semaphore()
    pairs = {
        "plan": (plan_hbm, plan_ref),
        "gain": (gain_hbm, gain),
        "arr": (arr_hbm.at[0], arr),
        "ex": (ex_hbm, ex),
        "stash0": (stash_hbm.at[0, :, 0:tok // 2], stash_low),
        "stash1": (stash_hbm.at[0, :, tok // 2:tok], stash_high),
        "gate": (gate_hbm.at[0], w1.at[:, 0:hidden]),
        "up": (up_hbm.at[0], w1.at[:, hidden:two_h]),
        "router": (router_hbm.at[0], w1.at[:, two_h:main]),
        "a": (a_hbm.at[0], a_t),
        "b": (b_hbm.at[0], b_ref),
        "fr": (froutes_hbm.at[0], froutes),
        "br": (broutes_hbm.at[0], broutes),
    }
    piece = width // PIECES
    for p in range(PIECES):
        cols = slice(p * piece, (p + 1) * piece)
        pairs["down%d" % p] = (down_hbm.at[0, :, cols], wd.at[:, cols])
        pairs["ret%d" % p] = (ret_hbm.at[0, :, cols], ret.at[:, cols])
    downs = ["down%d" % p for p in range(PIECES)]
    rets = ["ret%d" % p for p in range(PIECES)]
    loads = {
        name: pltpu.make_async_copy(a, b, load_sem.at[i])
        for i, (name, (a, b)) in enumerate(pairs.items())
    }

    def start(*names):
        for name in names:
            loads[name].start()

    def wait(*names):
        for name in names:
            loads[name].wait()

    def normalize(at, take, low=0, high=tok):
        def body(i, carry):
            rows = pl.ds(pl.multiple_of(low + i * ROWS, ROWS), ROWS)
            x = take(rows, pl.ds(pl.multiple_of(i * ROWS, ROWS), ROWS))
            x_buf[at, rows, :] = x
            r = lax.rsqrt(jnp.mean(x * x, axis=-1, keepdims=True) + 1e-6)
            n_buf[at, rows, :] = (x * r * gain[...]).astype(BF16)
            rs_buf[at, rows, :] = jnp.broadcast_to(r, (ROWS, rs_buf.shape[2]))
            return carry

        lax.fori_loop(0, (high - low) // ROWS, body, 0, unroll=True)

    def mark(at, routes):
        expert = lax.broadcasted_iota(jnp.int32, (experts, tok), 0)
        chosen = expert == routes[0:1, :]
        for k in range(1, routes.shape[0]):
            chosen = jnp.logical_or(chosen, expert == routes[k:k + 1, :])
        prob_buf[at] = jnp.where(chosen, 1.0, 0.0).T

    def project(at, first=False):
        n = n_buf[at]
        if first:
            wait("router", "gate")
        tail = dot(n, w1[:, two_h:full])
        logits = tail[:, 0:experts]
        low = tail[:, experts:experts + rank2].astype(BF16)
        low_buf[at] = low
        for j in range(two_h // TILE):
            cols = slice(j * TILE, (j + 1) * TILE)
            if j == 1:
                scores = jnp.where(prob_buf[at] > 0.5, jnp.exp(logits), 0.0)
                prob = scores / jnp.sum(scores, axis=-1, keepdims=True)
                prob_buf[at] = prob
                mean = jnp.sum(prob * logits, axis=-1, keepdims=True)
                ls_buf[at] = jnp.broadcast_to(logits[:, 0:1] - mean, ls_buf.shape[1:])
            if first and (j + 1) * TILE > hidden and j * TILE <= hidden:
                wait("up")
            pre[at, :, cols] = dot(n, w1[:, cols]) + 2.0 * dot(low, bd[:, cols])
        g = pre[at, :, 0:hidden]
        u = pre[at, :, hidden:two_h]
        sg = jax.nn.sigmoid(g)
        silu = g * sg
        h_buf[at] = (silu * u).astype(BF16)
        slope = u * (sg * (1.0 + g * (1.0 - sg)))
        pre[at, :, 0:hidden] = slope
        pre[at, :, hidden:two_h] = silu
        gc_buf[at] = slope * g + silu * u

    def send_y(t, p):
        cols = slice(p * piece, (p + 1) * piece)
        dst = fin.at[t, :, cols] if t < ticks - 1 else acts_out.at[0, :, cols]
        return pltpu.make_async_remote_copy(
            y_tx.at[t, :, cols], dst, y_send.at[t, p], y_recv.at[t, p],
            device_id={"section": lax.min(s + 1, sections - 1)}, device_id_type=MESH,
        )

    cuts = [0, LANES] + [p * piece for p in range(1, PIECES + 1)]
    parts_dx = len(cuts) - 1

    def send_dx(t, p):
        cols = slice(cuts[p], cuts[p + 1])
        dst = bin_.at[t, :, cols] if t < ticks - 1 else grads_out.at[0, :, cols]
        return pltpu.make_async_remote_copy(
            dx_tx.at[t, :, cols], dst, dx_send.at[t, p], dx_recv.at[t, p],
            device_id={"section": lax.max(s - 1, 0)}, device_id_type=MESH,
        )

    def turn(k):
        return lax.rem(place + k + 1, half)

    def to_partner(k):
        return pltpu.make_async_remote_copy(
            tot.at[(1 - side) * half + turn(k)], pair_rx.at[k], pair_send.at[k], pair_recv.at[k],
            device_id={"dp": partner}, device_id_type=MESH,
        )

    def to_peer(k):
        return pltpu.make_async_remote_copy(
            tot.at[side * half + turn(k)], peer_rx.at[k], peer_send.at[k], peer_recv.at[k],
            device_id={"dp": 2 * turn(k) + side}, device_id_type=MESH,
        )

    wa, wb = ga_out.shape[1], gb_out.shape[3]
    half_b = wb // 2
    a_rows = rank2 * (wa // LANES)

    def source(t, rows):
        arrived = arr[rows, :] if t == 0 else fin[t - 1, rows, :]
        return jnp.where(is_first, ex[t, rows, :].astype(F32), arrived)

    def prepare_forward(t):
        if t > 0:
            @pl.when(not_first)
            def _():
                for p in range(PIECES):
                    send_y(t - 1, p).wait_recv()

        mark(0, froutes[t])
        normalize(0, lambda rows, near: source(t, rows))

    def finish_forward(t):
        own = prob_buf[0, :, 0:1]
        for p in range(PIECES):
            cols = slice(p * piece, (p + 1) * piece)
            y_tx[t, :, cols] = x_buf[0, :, cols] + own * dot(h_buf[0], wd[:, cols])

            @pl.when(not_last)
            def _():
                send_y(t, p).start()

    def forward(t):
        prepare_forward(t)
        project(0)
        finish_forward(t)

    def prepare_recompute(t):
        slot = plan_ref[0, t]
        mark(1 + t, broutes[slot])
        for part, kept in enumerate((stash_low, stash_high)):
            if t == 0:
                wait("stash%d" % part)
            normalize(
                1 + t, lambda rows, near: kept[slot, near, :].astype(F32),
                part * (tok // 2), (part + 1) * (tok // 2),
            )

    def cotangent(t, cols):
        incoming = ret[:, cols] if t == 0 else bin_[t - 1, :, cols]
        return jnp.where(is_last, y_tx[t, :, cols] - ex[t, :, cols].astype(F32), incoming)

    def pulled(t, pieces):
        q = None
        for p in pieces:
            if t > 0:
                @pl.when(not_last)
                def _():
                    if p == 0:
                        send_dx(t - 1, 0).wait_recv()
                    send_dx(t - 1, p + 1).wait_recv()

            cols = slice(p * piece, (p + 1) * piece)
            part = dot_nt(cotangent(t, cols).astype(BF16), wd[:, cols])
            q = part if q is None else q + part
        return q

    def backward(t):
        kept = jnp.where(is_last, 0, 1 + t)

        if t == 0:
            @pl.when(fore_first)
            def _():
                q_buf[...] = pulled(0, range(EARLY))

            @pl.when(back_first)
            def _():
                wait(*downs[EARLY:], *rets[EARLY:])

            q = q_buf[...] + pulled(0, range(EARLY, PIECES))
        else:
            q = pulled(t, range(PIECES))
        prob = prob_buf[kept]
        own = prob[:, 0:1]
        d_own = jnp.sum(q * h_buf[kept].astype(F32), axis=-1, keepdims=True)
        d_hidden = own * q
        d_buf[:, 0:hidden] = (d_hidden * pre[kept, :, 0:hidden]).astype(BF16)
        d_buf[:, hidden:two_h] = (d_hidden * pre[kept, :, hidden:two_h]).astype(BF16)
        lane = lax.broadcasted_iota(jnp.int32, (tok, experts), 1)
        d_pick = d_own * own
        d_buf[:, two_h:main] = (d_pick * (jnp.where(lane == 0, 1.0, 0.0) - prob)).astype(BF16)
        inner = own * jnp.sum(q * gc_buf[kept], axis=-1, keepdims=True) + d_pick * ls_buf[kept, :, 0:1]
        r = rs_buf[kept, :, 0:1]
        corr[...] = jnp.broadcast_to(inner * r * r * (1.0 / width), corr.shape)
        d_low = (2.0 * dot_nt(d_buf[:, 0:two_h], bd[...])).astype(BF16)
        d_buf[:, main:full] = d_low

        def give(cols, m):
            dx_tx[t, :, cols] = (
                cotangent(t, cols) + rs_buf[kept, :, 0:1] * (m * gain[:, cols])
                - corr[:, 0:1] * x_buf[kept, :, cols]
            )

        head = slice(0, cuts[1])
        give(head, dot_nt(d_buf[:, 0:main], w1[head, 0:main]) + dot_nt(d_low, w1[head, main:full]))

        def gradients():
            grad_b = 2.0 * dot_tn(low_buf[kept], d_buf[:, 0:two_h])
            row = lax.broadcasted_iota(jnp.int32, (rank2, hidden), 0)
            grad_b = jnp.where(row < rank2 // 2, grad_b[:, 0:hidden], grad_b[:, hidden:two_h])
            grad_a = dot_tn(d_buf[:, main:full], n_buf[kept])
            entries = rank2 * width + rank2 * hidden
            square = jnp.sum(grad_a * grad_a) + jnp.sum(grad_b * grad_b)
            factor = lax.rsqrt(jnp.full((1, 1), square, F32) / entries + 1e-6) * (
                1.0 / (ticks * replicas)
            )
            grad_b = grad_b * factor
            both = jnp.concatenate([grad_b, pltpu.roll(grad_b, hidden - half_b, 1)], axis=0).T
            for n in range(replicas):
                block = (n % 2) * half + n // 2
                parts = [
                    (i * rank2, rank2, grad_a[:, c:c + LANES] * factor)
                    for i, c in enumerate(range(n * wa, (n + 1) * wa, LANES))
                ]
                parts.append((a_rows, half_b, both[n * wb:n * wb + half_b, :]))
                for at, count, value in parts:
                    if t == 0:
                        tot[block, at:at + count, :] = value
                    else:
                        tot[block, at:at + count, :] = tot[block, at:at + count, :] + value

        def spread():
            @pl.when(not_first)
            def _():
                for p in range(parts_dx):
                    for c in range(cuts[p], cuts[p + 1], TILE) if p > 0 else ():
                        cols = slice(c, min(c + TILE, cuts[p + 1]))
                        give(cols, dot_nt(d_buf[...], w1[cols, :]))
                    if t == 0 and p == 0:
                        @pl.when(back_first)
                        def _():
                            pl.semaphore_wait(barrier, half + 2)

                    send_dx(t, p).start()

        if t < ticks - 1:
            spread()
            gradients()
        else:
            gradients()
            for k in range(half):
                to_partner(k).start()
            spread()

    def exchange():
        for k in range(half):
            to_partner(k).wait_recv()
            block = side * half + turn(k)
            tot[block] = tot[block] + pair_rx[k]
            if k < half - 1:
                to_peer(k).start()

    start("gain", "a", "b")

    @pl.when(back_first)
    def _():
        start("plan", "br", *downs[:EARLY], *rets[:EARLY], "stash0", "stash1")

    @pl.when(fore_first)
    def _():
        start("fr")

        @pl.when(is_first)
        def _():
            start("ex")

        @pl.when(not_first)
        def _():
            start("arr")

    start("router", "gate", "up")

    @pl.when(back_first)
    def _():
        start(*downs[EARLY:], *rets[EARLY:])

    @pl.when(fore_first)
    def _():
        start(*downs)

    for d in (1, sections - 1):
        pl.semaphore_signal(
            barrier, inc=1, device_id={"section": lax.rem(s + d, sections)}, device_id_type=MESH
        )
    pl.semaphore_signal(barrier, inc=1, device_id={"dp": partner}, device_id_type=MESH)
    for d in range(1, half):
        pl.semaphore_signal(
            barrier, inc=1, device_id={"dp": lax.rem(me + 2 * d, replicas)}, device_id_type=MESH
        )

    bd[...] = jnp.zeros_like(bd)
    wait("gain", "a", "b")
    bd[0:rank2 // 2, 0:hidden] = b_ref[0]
    bd[rank2 // 2:rank2, hidden:two_h] = b_ref[1]
    w1[:, main:full] = a_t[...].astype(F32).T.astype(BF16)

    @pl.when(back_first)
    def _():
        wait(*downs[:EARLY], *rets[:EARLY])
        q_buf[...] = pulled(0, range(EARLY))
        wait("plan", "br")
        prepare_recompute(0)

    @pl.when(fore_first)
    def _():
        @pl.when(is_first)
        def _():
            wait("ex")

        @pl.when(not_first)
        def _():
            wait("arr")

        wait("fr")
        prepare_forward(0)

    project(jnp.where(back_first, 1, 0), first=True)

    @pl.when(back_first)
    def _():
        start("arr", "fr")

    @pl.when(fore_first)
    def _():
        @pl.when(not_last)
        def _():
            start("plan", "br", "stash0", "stash1", *rets)

        @pl.when(jnp.logical_and(is_last, not_first))
        def _():
            start("ex")

    @pl.when(fore_first)
    def _():
        wait(*downs)
        pl.semaphore_wait(barrier, half + 2)
        finish_forward(0)

        @pl.when(not_last)
        def _():
            wait("plan", "br", *rets)
            prepare_recompute(0)
            project(1)

        @pl.when(jnp.logical_and(is_last, not_first))
        def _():
            wait("ex")

    backward(0)

    @pl.when(back_first)
    def _():
        wait("arr", "fr")
        forward(0)

    edge_acts = pltpu.make_async_copy(zero, acts_out.at[0], zero_sem.at[0])
    edge_grads = pltpu.make_async_copy(zero, grads_out.at[0], zero_sem.at[0])
    at_edge = jnp.logical_or(is_first, is_last)

    @pl.when(at_edge)
    def _():
        zero[...] = jnp.zeros_like(zero)

    @pl.when(is_first)
    def _():
        edge_acts.start()

    @pl.when(jnp.logical_and(is_last, not_first))
    def _():
        edge_grads.start()

    for t in range(1, ticks):
        @pl.when(fore_first)
        def _():
            forward(t)

        @pl.when(not_last)
        def _():
            prepare_recompute(t)
            project(1 + t)

        backward(t)
        if t == ticks - 1:
            exchange()

        @pl.when(back_first)
        def _():
            forward(t)

    total = tot[side * half + place]
    for k in range(half - 1):
        to_peer(k).wait_recv()
        total = total + peer_rx[k]
    for i in range(wa // LANES):
        ga_out[:, i * LANES:(i + 1) * LANES] = total[i * rank2:(i + 1) * rank2, :]
    pad = jnp.zeros((LANES - half_b, LANES), F32)
    turned = jnp.concatenate([total[a_rows:a_rows + half_b, :], pad], axis=0).T
    lane = lax.broadcasted_iota(jnp.int32, (rank2, LANES), 1)
    sum_b = jnp.where(
        lane < half_b, turned[0:rank2, :], pltpu.roll(turned[rank2:2 * rank2, :], half_b, 1)
    )
    gb_out[0, 0] = sum_b[0:rank2 // 2, 0:wb]
    gb_out[0, 1] = sum_b[rank2 // 2:rank2, 0:wb]

    for k in range(half):
        to_partner(k).wait_send()
        if k < half - 1:
            to_peer(k).wait_send()

    @pl.when(not_first)
    def _():
        for p in range(PIECES):
            send_y(ticks - 1, p).wait_recv()
        for p in range(parts_dx):
            for t in range(ticks):
                send_dx(t, p).wait_send()

    @pl.when(not_last)
    def _():
        for p in range(PIECES):
            for t in range(ticks):
                send_y(t, p).wait_send()
        for p in range(parts_dx):
            send_dx(ticks - 1, p).wait_recv()

    @pl.when(is_first)
    def _():
        edge_acts.wait()

    @pl.when(jnp.logical_and(is_last, not_first))
    def _():
        edge_grads.wait()


def deliver(*refs):
    count = len(refs) // 2
    sem = refs[-1]
    copies = [
        pltpu.make_async_copy(refs[i], refs[count + i], sem.at[i]) for i in range(count)
    ]
    for copy in copies:
        copy.start()
    for copy in copies:
        copy.wait()


def shards(sections, replicas, *args):
    (examples, arriving, returning, stash, plan, forward_routes, backward_routes, gain,
     router, gate_w, up_w, down_w, down_factors, up_factors) = args
    ticks, tok, width = examples.shape
    hidden = gate_w.shape[2]
    experts = router.shape[2]
    rank2 = down_factors.shape[2]
    topk = forward_routes.shape[3]
    hbm = pl.BlockSpec(memory_space=pltpu.HBM)
    any_ = pl.BlockSpec(memory_space=pl.ANY)
    vmem = pl.BlockSpec(memory_space=pltpu.VMEM)
    wa, wb = width // replicas, hidden // replicas
    half = replicas // 2
    share = rank2 * (wa // LANES) + (wb // 2 + 7) // 8 * 8
    dma = pltpu.SemaphoreType.DMA
    vm = pltpu.VMEM
    outs = (
        jax.ShapeDtypeStruct((1, tok, width), F32),
        jax.ShapeDtypeStruct((1, tok, width), F32),
        jax.ShapeDtypeStruct((rank2, wa), F32),
        jax.ShapeDtypeStruct((1, 2, rank2 // 2, wb), F32),
    )
    operands = [
        pltpu.with_memory_space_constraint(value, pltpu.HBM)
        for value in (
            plan, examples, arriving, returning, stash, jnp.swapaxes(forward_routes, 2, 3),
            jnp.swapaxes(backward_routes, 2, 3), gain, router, gate_w, up_w, down_w,
            jnp.swapaxes(down_factors, 1, 2), up_factors,
        )
    ]
    results = pl.pallas_call(
        functools.partial(kernel, sections, replicas),
        out_shape=outs,
        in_specs=[hbm] * 14,
        out_specs=(any_, any_, vmem, vmem),
        scratch_shapes=[
            pltpu.SMEM((1, ticks), jnp.int32),
            vm((ticks, tok, width), BF16),
            vm((tok, width), F32),
            vm((tok, width), F32),
            vm((ticks, tok // 2, width), BF16),
            vm((ticks, tok // 2, width), BF16),
            vm((ticks, topk, tok), jnp.int32),
            vm((ticks, topk, tok), jnp.int32),
            vm((1, width), F32),
            vm((2, rank2 // 2, hidden), BF16),
            vm((width, 2 * hidden + experts + rank2), BF16),
            vm((hidden, width), BF16),
            vm((rank2, width), BF16),
            vm((rank2, 2 * hidden), BF16),
            vm((1 + ticks, tok, width), F32),
            vm((1 + ticks, tok, width), BF16),
            vm((1 + ticks, tok, LANES), F32),
            vm((1 + ticks, tok, 2 * hidden), F32),
            vm((1 + ticks, tok, hidden), BF16),
            vm((1 + ticks, tok, rank2), BF16),
            vm((1 + ticks, tok, experts), F32),
            vm((1 + ticks, tok, LANES), F32),
            vm((1 + ticks, tok, hidden), F32),
            vm((tok, hidden), F32),
            vm((tok, 2 * hidden + experts + rank2), BF16),
            vm((tok, LANES), F32),
            vm((ticks, tok, width), F32),
            vm((ticks, tok, width), F32),
            vm((ticks - 1, tok, width), F32),
            vm((ticks - 1, tok, width), F32),
            vm((replicas, share, LANES), F32),
            vm((half, share, LANES), F32),
            vm((half - 1, share, LANES), F32),
            vm((tok, width), F32),
            dma((13 + 2 * PIECES,)),
            dma((ticks, PIECES)),
            dma((ticks, PIECES)),
            dma((ticks, PIECES + 1)),
            dma((ticks, PIECES + 1)),
            dma((half,)),
            dma((half,)),
            dma((half - 1,)),
            dma((half - 1,)),
            dma((1,)),
        ],
        compiler_params=pltpu.CompilerParams(
            collective_id=0, has_side_effects=True, vmem_limit_bytes=44 * 1024 * 1024
        ),
    )(*operands)
    acts, grads, ga, gb = pl.pallas_call(
        deliver,
        out_shape=outs,
        in_specs=[any_] * 4,
        out_specs=(any_,) * 4,
        scratch_shapes=[dma((4,))],
        compiler_params=pltpu.CompilerParams(vmem_limit_bytes=1024 * 1024),
    )(*results)
    return acts, grads, ga.T[None], gb


def solution(mesh):
    in_specs = (
        P(None, "dp", None),
        P("section", "dp", None),
        P("section", "dp", None),
        P("section", None, "dp", None),
        P("section", None),
        P("section", None, "dp", None),
        P("section", None, "dp", None),
        P("section", None),
        P("section", None, None),
        P("section", None, None),
        P("section", None, None),
        P("section", None, None),
        P("section", None, None),
        P("section", None, None, None),
    )
    out_specs = (
        P("section", "dp", None),
        P("section", "dp", None),
        P("section", "dp", None),
        P("section", None, None, "dp"),
    )
    body = functools.partial(shards, mesh.shape["section"], mesh.shape["dp"])
    return jax.shard_map(body, mesh=mesh, in_specs=in_specs, out_specs=out_specs, check_vma=False)
```
